256 devices in a mesh: region: 16 (over z_lo, x, core), member: 16 (over y, z_hi).
Axes of the slice: x: 4, y: 4, z: 8 (z_hi: 4, z_lo: 2; z = z_hi * 2 + z_lo), core: 2. Of those that a mesh axis runs over, the one named last changes fastest.
Arguments:
- predicted_states: float32 [32, 100, 512, 128], P('member', None, 'region'), may hold values from -20 to 20, as said below
- observed_analysis: float32 [100, 512, 128], P(None, 'region'), may hold values from -20 to 20
- tile_location_sequence: int32 [16, 4096], P('region'), may hold values from 0 to 4095, each once within a row
Outputs:
- gradient: float32 [32, 100, 512, 128], P('member', None, 'region')
The draws below stay inside these ranges and needn't reach their ends.
Inputs may be any that keep to these rules, and one draw needn't show every extreme that they name: Each row of tile_location_sequence is a permutation of the cells of one region. `predicted_states`: members share a common field per variable and cell, with variable and cell scales.
All inputs are finite; a program needn't handle non-finite values.
Results may differ from the reference program's by a relative error of at most 0.0003.
Values sent between devices are 32-bit elements; how exact they have to be, the bound alone decides.
A program may use at most 128 MiB of HBM per device.

```python
import jax
import jax.numpy as jnp
from jax import lax

V = 100
ROWS_DEV = 32
LON = 128
HALF = 32
PATCH = 128
MEMBERS = 32
REGIONS = 16
ROWS = 512
N_REGION = 16


def shared_parts(key):
    base = jax.random.fold_in(key, 101)
    first_key, second_key, third_key = jax.random.split(base, 3)
    common = jax.random.normal(first_key, (V, ROWS, LON), jnp.float32)
    var_scale = jnp.exp(jax.random.uniform(second_key, (V, 1, 1), jnp.float32, -1.15, 1.15))
    cell_scale = jnp.exp(jax.random.uniform(third_key, (1, ROWS, LON), jnp.float32, -0.7, 0.7))
    return (common, var_scale * cell_scale)


def draw_predicted_states(key, part):
    common, scales = shared_parts(key)
    noise = jax.random.normal(jax.random.fold_in(key, 202), (MEMBERS, V, ROWS, LON), jnp.float32)
    return jnp.clip(scales[None] * (common[None] + 0.6 * noise), -20.0, 20.0)


def draw_observed_analysis(key, part):
    common, scales = shared_parts(key)
    noise = jax.random.normal(jax.random.fold_in(key, 303), (V, ROWS, LON), jnp.float32)
    return jnp.clip(scales * (common + 0.6 * noise), -20.0, 20.0)


def setup_inputs(seed: int = 0) -> dict:
    arg_keys = jax.random.split(jax.random.key(seed), 4)
    return {
        "predicted_states": draw_predicted_states(jax.random.fold_in(arg_keys[3], 71), 0),
        "observed_analysis": draw_observed_analysis(jax.random.fold_in(arg_keys[3], 71), 0),
        "tile_location_sequence": jax.vmap(lambda own: jax.random.permutation(own, ROWS_DEV * LON))(jax.random.split(arg_keys[2], REGIONS)).reshape((REGIONS, ROWS_DEV * LON)).astype(jnp.int32),
    }


def kernel_value(offset, half):
    sigma = half / 2.0
    steps = jnp.arange(-half, half + 1).astype(jnp.float32)
    norm_sum = jnp.sum(jnp.exp(-(steps * steps) / (2.0 * sigma * sigma)))
    bell = jnp.exp(-(offset * offset) / (2.0 * sigma * sigma)) / norm_sum
    value = 0.5 * (offset == 0.0).astype(jnp.float32) + 0.5 * bell
    return jnp.where(jnp.abs(offset) <= half, value, jnp.zeros_like(value))

def lon_matrix():
    first = jnp.arange(LON)[:, None]
    second = jnp.arange(LON)[None, :]
    offset = second - first
    return kernel_value(offset.astype(jnp.float32), HALF)

def smooth_surface(values):
    along_lon = jnp.einsum('mrl,lk->mrk', values, lon_matrix(), precision=lax.Precision.HIGHEST)
    padded = jnp.pad(along_lon, ((0, 0), (HALF, HALF), (0, 0)))
    result = jnp.zeros_like(along_lon)
    for offset in range(-HALF, HALF + 1):
        weight = kernel_value(jnp.float32(offset), HALF)
        result = result + weight * padded[:, HALF + offset:HALF + offset + ROWS, :]
    return result

def reference(predicted_states, observed_analysis, tile_location_sequence):
    mesh_locations = ROWS_DEV * LON
    blocks = mesh_locations // PATCH
    region_index = jnp.arange(N_REGION).astype(jnp.int32)[:, None]

    def lone_quantity(pair):
        members_field, truth = pair
        softened_surface = smooth_surface(members_field)
        by_region = softened_surface.reshape(MEMBERS, N_REGION, mesh_locations)
        picked = by_region[:, region_index, tile_location_sequence].reshape(MEMBERS, N_REGION * blocks, PATCH)
        truth_picked = truth.reshape(N_REGION, mesh_locations)[region_index, tile_location_sequence].reshape(N_REGION * blocks, PATCH)
        diff = picked - truth_picked[None]
        toward = diff / jnp.sqrt(lax.optimization_barrier(jnp.sum(diff * diff, axis=-1, keepdims=True)) + 1e-06)
        inner_products = jnp.einsum('mkp,nkp->kmn', picked, picked, precision=lax.Precision.HIGHEST)
        squares = jnp.einsum('mkp,mkp->km', picked, picked, precision=lax.Precision.HIGHEST)
        dist_sq = jnp.maximum(squares[:, :, None] + squares[:, None, :] - 2.0 * inner_products, 0.0)
        self_pair = jnp.arange(MEMBERS)[:, None] == jnp.arange(MEMBERS)[None, :]
        pair_weights = jnp.where(self_pair[None], jnp.zeros_like(dist_sq), 1.0 / jnp.sqrt(dist_sq + 1e-06))
        pulled = lax.optimization_barrier(jnp.sum(pair_weights, axis=-1)).T
        apart = pulled[:, :, None] * picked - jnp.einsum('kmn,nkp->mkp', pair_weights, picked, precision=lax.Precision.HIGHEST)
        apart = apart / MEMBERS
        patch_grad = jnp.sqrt(jnp.float32(PATCH)) * (toward - apart)
        located_points = jnp.zeros((MEMBERS, N_REGION, mesh_locations), jnp.float32)
        located_points = located_points.at[:, region_index, tile_location_sequence].set(patch_grad.reshape(MEMBERS, N_REGION, mesh_locations))
        return smooth_surface(located_points.reshape(MEMBERS, ROWS, LON))
    layered_surfaces = lax.map(lone_quantity, (jnp.transpose(predicted_states, (1, 0, 2, 3)), observed_analysis))
    return jnp.transpose(layered_surfaces, (1, 0, 2, 3))
```

```python
import math

import jax
import jax.numpy as jnp
import numpy as np
from jax import lax
from jax.experimental import pallas as pl
from jax.experimental.pallas import tpu as pltpu
from jax.sharding import PartitionSpec as P

V = 100
ROWS = 32
LON = 128
HALF = 32
PATCH = 128
MEMBERS = 32
OWNERS = 16
REGIONS = 16
SLOTS = 7
SPAN = ROWS + 2 * HALF
CELLS = ROWS * LON
MESH = pl.DeviceIdType.MESH
F32 = jnp.float32
BF16 = jnp.bfloat16


def kernel_values(offset):
    sigma = HALF / 2.0
    steps = np.arange(-HALF, HALF + 1).astype(np.float64)
    norm = np.sum(np.exp(-(steps * steps) / (2.0 * sigma * sigma)))
    bell = np.exp(-(offset * offset) / (2.0 * sigma * sigma)) / norm
    value = 0.5 * (offset == 0.0) + 0.5 * bell
    return np.where(np.abs(offset) <= HALF, value, 0.0).astype(np.float32)


def halves(values):
    high = values.astype(BF16)
    low = (values - high.astype(np.float32)).astype(BF16)
    return high, low


def lat_weights():
    rows = np.arange(ROWS)[:, None]
    span = np.arange(SPAN)[None, :]
    high, low = halves(kernel_values((span - HALF - rows).astype(np.float64)))
    return np.concatenate(
        [np.concatenate([high, high], 1), np.concatenate([low, np.zeros_like(low)], 1)], 0
    )


def lon_weights():
    first = np.arange(LON)[:, None]
    second = np.arange(LON)[None, :]
    high, low = halves(kernel_values((second - first).astype(np.float64)))
    return np.concatenate(
        [np.concatenate([high, low], 1), np.concatenate([high, np.zeros_like(low)], 1)], 0
    )


def split(values):
    high = values.astype(BF16)
    low = (values - high.astype(F32)).astype(BF16)
    return high, low


def dot(a, b):
    return lax.dot_general(a, b, (((1,), (0,)), ((), ())), preferred_element_type=F32)


def dot_nt(a, b):
    return lax.dot_general(a, b, (((1,), (1,)), ((), ())), preferred_element_type=F32)


LANES = lax.GatherDimensionNumbers(
    offset_dims=(),
    collapsed_slice_dims=(1,),
    start_index_map=(1,),
    operand_batching_dims=(0,),
    start_indices_batching_dims=(0,),
)


def take_lanes(values, lanes):
    return lax.gather(
        values,
        lanes[..., None],
        LANES,
        slice_sizes=(1, 1),
        mode=lax.GatherScatterMode.PROMISE_IN_BOUNDS,
    )


def pick(src, group, row_of, lane_of, index):
    lanes = jnp.broadcast_to(lane_of[pl.ds(index, 1), :], (group, LON))
    rows = jnp.broadcast_to(row_of[pl.ds(index, 1), :], (group, LON))
    total = jnp.zeros((group, LON), F32)
    for row in range(ROWS):
        found = take_lanes(src[pl.ds(row * group, group), :], lanes)
        total = jnp.where(rows == row, found, total)
    return total


def smooth_lat(field, lat, mid):
    def pair(index, carry):
        both = jnp.concatenate([field[2 * index], field[2 * index + 1]], axis=1)
        high, low = split(both)
        parts = dot(lat[...], jnp.concatenate([high, low], axis=0))
        rows = parts[:ROWS] + parts[ROWS:]
        mid[pl.ds(pl.multiple_of(2 * index * ROWS, 64), ROWS), :] = rows[:, :LON]
        mid[pl.ds(pl.multiple_of(2 * index * ROWS + ROWS, 32), ROWS), :] = rows[:, LON:]
        return carry

    lax.fori_loop(0, MEMBERS // 2, pair, 0, unroll=2)


def smooth_lon(block, lon):
    high, low = split(block)
    parts = dot(jnp.concatenate([high, low], axis=1), lon[...])
    return parts[:, :LON] + parts[:, LON:]


def pair_block(a, truths):
    count = 4
    cube = a.reshape(count, MEMBERS, PATCH)
    mean = jnp.sum(cube, axis=1, keepdims=True) * (1.0 / MEMBERS)
    e = (cube - mean).reshape(count * MEMBERS, PATCH)
    d = (cube - truths).reshape(count * MEMBERS, PATCH)
    toward = d * lax.rsqrt(jnp.sum(d * d, axis=1, keepdims=True) + 1e-06)
    size = count * MEMBERS
    left = lax.broadcasted_iota(jnp.int32, (size, size), 0)
    right = lax.broadcasted_iota(jnp.int32, (size, size), 1)
    same = left == right
    other = jnp.logical_and(lax.div(left, MEMBERS) == lax.div(right, MEMBERS), left != right)
    high, low = split(e)
    gram = dot_nt(jnp.concatenate([high, low], axis=1), jnp.concatenate([high, high], axis=1))
    gram = gram + dot_nt(high, low)
    diagonal = jnp.where(same, gram, 0.0)
    dist = jnp.sum(diagonal, axis=1, keepdims=True) + jnp.sum(diagonal, axis=0, keepdims=True)
    dist = jnp.maximum(dist - 2.0 * gram, 0.0)
    weights = jnp.where(other, lax.rsqrt(dist + 1e-06), 0.0)
    pulled = jnp.sum(weights, axis=1, keepdims=True)
    mixing = jnp.where(same, pulled, -weights)
    mix_high, mix_low = split(mixing)
    apart = dot(jnp.concatenate([mix_high, mix_low], axis=1), jnp.concatenate([high, high], axis=0))
    apart = apart + dot(mix_high, low)
    return math.sqrt(PATCH) * (toward - apart * (1.0 / MEMBERS))


def kernel(
    x, truth, order, lat, lon, out,
    raw, grad, done, mid, cells, picked, facts, fact_rows, rows_fwd, lanes_fwd, rows_inv, lanes_inv,
    fwd_send, fwd_recv, up_send, up_recv, down_send, down_recv,
    up2_send, up2_recv, down2_send, down2_recv, ret_send, ret_recv, fact_sem,
):
    r = lax.axis_index("region")
    m = lax.axis_index("member")
    slots = jnp.where(lax.rem(m, 5) == 0, SLOTS, SLOTS - 1)
    has_low = r > 0
    has_high = r < REGIONS - 1

    def variable(slot, owner):
        return jnp.where(slot == SLOTS - 1, 96 + lax.div(owner, 5), slot * OWNERS + owner)

    barrier = pltpu.get_barrier_semaphore()
    for step in range(1, OWNERS):
        peer = (r, lax.rem(m + step, OWNERS))
        pl.semaphore_signal(barrier, inc=1, device_id=peer, device_id_type=MESH)

    @pl.when(has_low)
    def _():
        pl.semaphore_signal(barrier, inc=1, device_id=(r - 1, m), device_id_type=MESH)

    @pl.when(has_high)
    def _():
        pl.semaphore_signal(barrier, inc=1, device_id=(r + 1, m), device_id_type=MESH)

    pl.semaphore_wait(barrier, OWNERS - 1 + has_low.astype(jnp.int32) + has_high.astype(jnp.int32))

    def own_rows(slot):
        return raw.at[slot, pl.ds(2 * m, 2), pl.ds(HALF, ROWS), :]

    def send_block(slot, peer):
        pltpu.make_async_remote_copy(
            src_ref=x.at[:, variable(slot, peer)],
            dst_ref=own_rows(slot),
            send_sem=fwd_send,
            recv_sem=fwd_recv.at[slot],
            device_id=(r, peer),
            device_id_type=MESH,
        ).start()

    def send_slot(slot, carry):
        def to_peer(step, inner):
            send_block(slot, lax.rem(m + step, OWNERS))
            return inner

        return lax.fori_loop(1, OWNERS, to_peer, carry)

    lax.fori_loop(0, SLOTS - 1, send_slot, 0)
    for index in range(4):

        @pl.when(m != 5 * index)
        def _(index=index):
            send_block(SLOTS - 1, 5 * index)

    def keep_slot(slot, carry):
        pltpu.make_async_copy(x.at[:, variable(slot, m)], own_rows(slot), fwd_recv.at[slot]).start()
        pltpu.make_async_copy(truth.at[variable(slot, m)], facts.at[slot], fact_sem).start()
        return carry

    lax.fori_loop(0, slots, keep_slot, 0)

    def invert(k, carry):
        cell = order[pl.ds(k, 1), :]
        row = lax.shift_right_logical(cell, 7)
        lane = jnp.bitwise_and(cell, LON - 1)
        rows_fwd[pl.ds(k, 1), :] = row
        lanes_fwd[pl.ds(k, 1), :] = lane
        at_row = lax.broadcasted_iota(jnp.int32, (ROWS, PATCH), 0) == row
        position = lax.broadcasted_iota(jnp.int32, (ROWS, PATCH), 1).astype(F32)
        patch = jnp.where(at_row, k.astype(F32), 0.0)
        place = jnp.where(at_row, position, 0.0)
        at_lane = lax.broadcasted_iota(jnp.int32, (LON, PATCH), 0) == lane
        chosen = jnp.where(at_lane, 1.0, 0.0).astype(BF16)
        return carry + dot_nt(jnp.concatenate([patch, place], axis=0).astype(BF16), chosen)

    inverse = lax.fori_loop(0, ROWS, invert, jnp.zeros((2 * ROWS, LON), F32))
    inverse = inverse.astype(jnp.int32)
    rows_inv[...] = inverse[:ROWS]
    lanes_inv[...] = inverse[ROWS:]

    @pl.when(slots == SLOTS)
    def _():
        pltpu.make_async_copy(facts.at[pl.ds(0, 7)], facts.at[pl.ds(0, 7)], fact_sem).wait()

    @pl.when(slots != SLOTS)
    def _():
        pltpu.make_async_copy(facts.at[pl.ds(0, 6)], facts.at[pl.ds(0, 6)], fact_sem).wait()

    for row in range(ROWS):
        fact_rows[pl.ds(row * 8, 8), :] = facts[:, row, :]

    def pick_fact(k, carry):
        picked[pl.ds(pl.multiple_of(k * 8, 8), 8), :] = pick(fact_rows, 8, rows_fwd, lanes_fwd, k)
        return carry

    lax.fori_loop(0, ROWS, pick_fact, 0)
    fact_rows[...] = picked[pl.ds(0, 8 * ROWS), :]

    @pl.when(jnp.logical_not(has_low))
    def _():
        def clear(slot, carry):
            raw[slot, :, pl.ds(0, HALF), :] = jnp.zeros((MEMBERS, HALF, LON), F32)
            grad[slot, :, pl.ds(0, HALF), :] = jnp.zeros((MEMBERS, HALF, LON), F32)
            return carry

        lax.fori_loop(0, slots, clear, 0)

    @pl.when(jnp.logical_not(has_high))
    def _():
        def clear(slot, carry):
            raw[slot, :, pl.ds(HALF + ROWS, HALF), :] = jnp.zeros((MEMBERS, HALF, LON), F32)
            grad[slot, :, pl.ds(HALF + ROWS, HALF), :] = jnp.zeros((MEMBERS, HALF, LON), F32)
            return carry

        lax.fori_loop(0, slots, clear, 0)

    def send_halos(field, slot, low_send, low_recv, high_send, high_recv):
        middle = field.at[slot, :, pl.ds(HALF, ROWS), :]

        @pl.when(has_high)
        def _():
            pltpu.make_async_remote_copy(
                src_ref=middle,
                dst_ref=field.at[slot, :, pl.ds(0, HALF), :],
                send_sem=high_send,
                recv_sem=high_recv.at[slot],
                device_id=(r + 1, m),
                device_id_type=MESH,
            ).start()

        @pl.when(has_low)
        def _():
            pltpu.make_async_remote_copy(
                src_ref=middle,
                dst_ref=field.at[slot, :, pl.ds(HALF + ROWS, HALF), :],
                send_sem=low_send,
                recv_sem=low_recv.at[slot],
                device_id=(r - 1, m),
                device_id_type=MESH,
            ).start()

    def wait_halos(field, slot, low_recv, high_recv):
        @pl.when(has_low)
        def _():
            part = field.at[slot, :, pl.ds(0, HALF), :]
            pltpu.make_async_copy(part, part, high_recv.at[slot]).wait()

        @pl.when(has_high)
        def _():
            part = field.at[slot, :, pl.ds(HALF + ROWS, HALF), :]
            pltpu.make_async_copy(part, part, low_recv.at[slot]).wait()

    def arrive(slot):
        part = raw.at[slot, :, pl.ds(HALF, ROWS), :]
        pltpu.make_async_copy(part, part, fwd_recv.at[slot]).wait()
        send_halos(raw, slot, down_send, down_recv, up_send, up_recv)

    def middle(slot):
        wait_halos(raw, slot, down_recv, up_recv)
        smooth_lat(raw.at[slot], lat, mid)
        for block in range(4):
            rows = [mid[pl.ds(block * 8 + row, MEMBERS, stride=ROWS), :] for row in range(8)]
            cells[pl.ds(block * 256, 256), :] = smooth_lon(jnp.concatenate(rows, axis=0), lon)

        def pick_patch(k, carry):
            at = pl.multiple_of(k * MEMBERS, MEMBERS)
            picked[pl.ds(at, MEMBERS), :] = pick(cells, MEMBERS, rows_fwd, lanes_fwd, k)
            return carry

        lax.fori_loop(0, ROWS, pick_patch, 0)

        def quad(q, carry):
            at = pl.multiple_of(q * 4 * MEMBERS, 4 * MEMBERS)
            truths = jnp.stack(
                [fact_rows[pl.ds((4 * q + i) * 8 + slot, 1), :] for i in range(4)], axis=0
            )
            cells[pl.ds(at, 4 * MEMBERS), :] = pair_block(picked[pl.ds(at, 4 * MEMBERS), :], truths)
            return carry

        lax.fori_loop(0, ROWS // 4, quad, 0)

        def put_row(row, carry):
            grad[slot, :, HALF + row, :] = pick(cells, MEMBERS, rows_inv, lanes_inv, row)
            return carry

        lax.fori_loop(0, ROWS, put_row, 0)

    def finish(slot):
        wait_halos(grad, slot, down2_recv, up2_recv)
        smooth_lat(grad.at[slot], lat, mid)
        for block in range(4):
            part = smooth_lon(mid[pl.ds(block * 256, 256), :], lon)
            done[slot, pl.ds(block * 8, 8)] = part.reshape(8, ROWS, LON)

    def give_back(slot):
        def to_peer(step, carry):
            peer = lax.rem(m + step, OWNERS)
            pltpu.make_async_remote_copy(
                src_ref=done.at[slot, pl.ds(2 * peer, 2)],
                dst_ref=out.at[:, variable(slot, m)],
                send_sem=ret_send,
                recv_sem=ret_recv,
                device_id=(r, peer),
                device_id_type=MESH,
            ).start()
            return carry

        lax.fori_loop(1, OWNERS, to_peer, 0)
        pltpu.make_async_copy(
            done.at[slot, pl.ds(2 * m, 2)], out.at[:, variable(slot, m)], ret_recv
        ).start()

    def step(i, carry):
        @pl.when(jnp.logical_and(i >= 3, i < slots + 3))
        def _():
            give_back(i - 3)

        @pl.when(i < slots)
        def _():
            arrive(i)

        @pl.when(jnp.logical_and(i >= 1, i < slots + 1))
        def _():
            middle(i - 1)

        @pl.when(jnp.logical_and(i >= 2, i < slots + 2))
        def _():
            finish(i - 2)

        @pl.when(jnp.logical_and(i >= 1, i < slots + 1))
        def _():
            send_halos(grad, i - 1, down2_send, down2_recv, up2_send, up2_recv)

        return carry

    lax.fori_loop(0, SLOTS + 3, step, 0)

    def drain(count):
        pltpu.make_async_copy(
            x.at[:, pl.ds(0, V - count)], x.at[:, pl.ds(0, V - count)], fwd_send
        ).wait()
        sent = done.at[pl.ds(0, count), pl.ds(0, 2 * OWNERS - 2)]
        pltpu.make_async_copy(sent, sent, ret_send).wait()

        @pl.when(has_high)
        def _():
            for field, sem in ((raw, up_send), (grad, up2_send)):
                part = field.at[pl.ds(0, count), :, pl.ds(HALF, ROWS), :]
                pltpu.make_async_copy(part, part, sem).wait()

        @pl.when(has_low)
        def _():
            for field, sem in ((raw, down_send), (grad, down2_send)):
                part = field.at[pl.ds(0, count), :, pl.ds(HALF, ROWS), :]
                pltpu.make_async_copy(part, part, sem).wait()

    @pl.when(slots == SLOTS)
    def _():
        drain(SLOTS)

    @pl.when(slots != SLOTS)
    def _():
        drain(SLOTS - 1)

    pltpu.make_async_copy(out, out, ret_recv).wait()


def on_device(predicted_states, observed_analysis, tile_location_sequence):
    order = tile_location_sequence.reshape(ROWS, PATCH)
    dma = pltpu.SemaphoreType.DMA
    vmem = pl.BlockSpec(memory_space=pltpu.VMEM)
    hbm = pl.BlockSpec(memory_space=pl.ANY)
    return pl.pallas_call(
        kernel,
        out_shape=jax.ShapeDtypeStruct((2, V, ROWS, LON), F32),
        in_specs=[hbm, hbm, vmem, vmem, vmem],
        out_specs=hbm,
        scratch_shapes=[
            pltpu.VMEM((SLOTS, MEMBERS, SPAN, LON), F32),
            pltpu.VMEM((SLOTS, MEMBERS, SPAN, LON), F32),
            pltpu.VMEM((SLOTS, MEMBERS, ROWS, LON), F32),
            pltpu.VMEM((MEMBERS * ROWS, LON), F32),
            pltpu.VMEM((MEMBERS * ROWS, LON), F32),
            pltpu.VMEM((MEMBERS * ROWS, LON), F32),
            pltpu.VMEM((8, ROWS, LON), F32),
            pltpu.VMEM((8 * ROWS, LON), F32),
            pltpu.VMEM((ROWS, LON), jnp.int32),
            pltpu.VMEM((ROWS, LON), jnp.int32),
            pltpu.VMEM((ROWS, LON), jnp.int32),
            pltpu.VMEM((ROWS, LON), jnp.int32),
            dma(()), dma((SLOTS,)), dma(()), dma((SLOTS,)), dma(()), dma((SLOTS,)),
            dma(()), dma((SLOTS,)), dma(()), dma((SLOTS,)), dma(()), dma(()), dma(()),
        ],
        compiler_params=pltpu.CompilerParams(
            collective_id=0, has_side_effects=True, vmem_limit_bytes=56 * 1024 * 1024
        ),
    )(
        predicted_states,
        observed_analysis,
        order,
        jnp.asarray(lat_weights()),
        jnp.asarray(lon_weights()),
    )


def solution(mesh):
    in_specs = (P("member", None, "region", None), P(None, "region", None), P("region", None))
    out_specs = P("member", None, "region", None)
    return jax.shard_map(
        on_device, mesh=mesh, in_specs=in_specs, out_specs=out_specs, check_vma=False
    )
```

```python
import math

import jax
import jax.numpy as jnp
import numpy as np
from jax import lax
from jax.experimental import pallas as pl
from jax.experimental.pallas import tpu as pltpu
from jax.sharding import PartitionSpec as P

V = 100
ROWS = 32
LON = 128
HALF = 32
PATCH = 128
MEMBERS = 32
OWNERS = 16
REGIONS = 16
SLOTS = 7
SPAN = ROWS + 2 * HALF
CELLS = ROWS * LON
MESH = pl.DeviceIdType.MESH
F32 = jnp.float32
BF16 = jnp.bfloat16


def kernel_values(offset):
    sigma = HALF / 2.0
    steps = np.arange(-HALF, HALF + 1).astype(np.float64)
    norm = np.sum(np.exp(-(steps * steps) / (2.0 * sigma * sigma)))
    bell = np.exp(-(offset * offset) / (2.0 * sigma * sigma)) / norm
    value = 0.5 * (offset == 0.0) + 0.5 * bell
    return np.where(np.abs(offset) <= HALF, value, 0.0).astype(np.float32)


def halves(values):
    high = values.astype(BF16)
    low = (values - high.astype(np.float32)).astype(BF16)
    return high, low


def lat_weights():
    rows = np.arange(ROWS)[:, None]
    span = np.arange(SPAN)[None, :]
    high, low = halves(kernel_values((span - HALF - rows).astype(np.float64)))
    return np.concatenate(
        [np.concatenate([high, high], 1), np.concatenate([low, np.zeros_like(low)], 1)], 0
    )


def lon_weights():
    first = np.arange(LON)[:, None]
    second = np.arange(LON)[None, :]
    high, low = halves(kernel_values((second - first).astype(np.float64)))
    return np.concatenate(
        [np.concatenate([high, low], 1), np.concatenate([high, np.zeros_like(low)], 1)], 0
    )


def split(values):
    high = values.astype(BF16)
    low = (values - high.astype(F32)).astype(BF16)
    return high, low


def dot(a, b):
    return lax.dot_general(a, b, (((1,), (0,)), ((), ())), preferred_element_type=F32)


def dot_nt(a, b):
    return lax.dot_general(a, b, (((1,), (1,)), ((), ())), preferred_element_type=F32)


LANES = lax.GatherDimensionNumbers(
    offset_dims=(),
    collapsed_slice_dims=(1,),
    start_index_map=(1,),
    operand_batching_dims=(0,),
    start_indices_batching_dims=(0,),
)


def take_lanes(values, lanes):
    return lax.gather(
        values,
        lanes[..., None],
        LANES,
        slice_sizes=(1, 1),
        mode=lax.GatherScatterMode.PROMISE_IN_BOUNDS,
    )


def pick(src, group, row_of, lane_of, index):
    lanes = jnp.broadcast_to(lane_of[pl.ds(index, 1), :], (group, LON))
    rows = jnp.broadcast_to(row_of[pl.ds(index, 1), :], (group, LON))
    total = jnp.zeros((group, LON), F32)
    for row in range(ROWS):
        found = take_lanes(src[pl.ds(row * group, group), :], lanes)
        total = jnp.where(rows == row, found, total)
    return total


def smooth_lat(field, lat, mid):
    def pair(index, carry):
        both = jnp.concatenate([field[2 * index], field[2 * index + 1]], axis=1)
        high, low = split(both)
        parts = dot(lat[...], jnp.concatenate([high, low], axis=0))
        rows = parts[:ROWS] + parts[ROWS:]
        mid[pl.ds(pl.multiple_of(2 * index * ROWS, 64), ROWS), :] = rows[:, :LON]
        mid[pl.ds(pl.multiple_of(2 * index * ROWS + ROWS, 32), ROWS), :] = rows[:, LON:]
        return carry

    lax.fori_loop(0, MEMBERS // 2, pair, 0, unroll=2)


def smooth_lon(block, lon):
    high, low = split(block)
    parts = dot(jnp.concatenate([high, low], axis=1), lon[...])
    return parts[:, :LON] + parts[:, LON:]


def pair_block(a, truths):
    count = 4
    cube = a.reshape(count, MEMBERS, PATCH)
    mean = jnp.sum(cube, axis=1, keepdims=True) * (1.0 / MEMBERS)
    e = (cube - mean).reshape(count * MEMBERS, PATCH)
    d = (cube - truths).reshape(count * MEMBERS, PATCH)
    toward = d * lax.rsqrt(jnp.sum(d * d, axis=1, keepdims=True) + 1e-06)
    size = count * MEMBERS
    left = lax.broadcasted_iota(jnp.int32, (size, size), 0)
    right = lax.broadcasted_iota(jnp.int32, (size, size), 1)
    same = left == right
    other = jnp.logical_and(lax.div(left, MEMBERS) == lax.div(right, MEMBERS), left != right)
    high, low = split(e)
    gram = dot_nt(jnp.concatenate([high, low], axis=1), jnp.concatenate([high, high], axis=1))
    gram = gram + dot_nt(high, low)
    diagonal = jnp.where(same, gram, 0.0)
    dist = jnp.sum(diagonal, axis=1, keepdims=True) + jnp.sum(diagonal, axis=0, keepdims=True)
    dist = jnp.maximum(dist - 2.0 * gram, 0.0)
    weights = jnp.where(other, lax.rsqrt(dist + 1e-06), 0.0)
    pulled = jnp.sum(weights, axis=1, keepdims=True)
    mixing = jnp.where(same, pulled, -weights)
    mix_high, mix_low = split(mixing)
    apart = dot(jnp.concatenate([mix_high, mix_low], axis=1), jnp.concatenate([high, high], axis=0))
    apart = apart + dot(mix_high, low)
    return math.sqrt(PATCH) * (toward - apart * (1.0 / MEMBERS))


def kernel(
    x, truth, order, lat, lon, out,
    raw, grad, done, mid, cells, picked, facts, fact_rows, rows_fwd, lanes_fwd, rows_inv, lanes_inv,
    fwd_send, fwd_recv, up_send, up_recv, down_send, down_recv,
    up2_send, up2_recv, down2_send, down2_recv, ret_send, ret_recv, fact_sem,
):
    r = lax.axis_index("region")
    m = lax.axis_index("member")
    slots = jnp.where(lax.rem(m, 5) == 0, SLOTS, SLOTS - 1)
    has_low = r > 0
    has_high = r < REGIONS - 1

    def turned(owner, by):
        return lax.div(owner, 4) * 4 + lax.rem(owner + 4 + by, 4)

    def variable(slot, owner):
        back = jnp.logical_and(lax.rem(slot, 2) == 1, r >= REGIONS // 2)
        place = jnp.where(back, turned(owner, 1), owner)
        return jnp.where(slot == SLOTS - 1, 96 + lax.div(owner, 5), slot * OWNERS + place)

    def above(slot):
        cross = jnp.logical_and(lax.rem(slot, 2) == 1, r == REGIONS // 2 - 1)
        return (r + 1, jnp.where(cross, turned(m, -1), m))

    def below(slot):
        cross = jnp.logical_and(lax.rem(slot, 2) == 1, r == REGIONS // 2)
        return (r - 1, jnp.where(cross, turned(m, 1), m))

    barrier = pltpu.get_barrier_semaphore()
    for step in range(1, OWNERS):
        peer = (r, lax.rem(m + step, OWNERS))
        pl.semaphore_signal(barrier, inc=1, device_id=peer, device_id_type=MESH)

    @pl.when(has_low)
    def _():
        pl.semaphore_signal(barrier, inc=1, device_id=(r - 1, m), device_id_type=MESH)

    @pl.when(has_high)
    def _():
        pl.semaphore_signal(barrier, inc=1, device_id=(r + 1, m), device_id_type=MESH)

    @pl.when(r == REGIONS // 2 - 1)
    def _():
        pl.semaphore_signal(barrier, inc=1, device_id=above(1), device_id_type=MESH)

    @pl.when(r == REGIONS // 2)
    def _():
        pl.semaphore_signal(barrier, inc=1, device_id=below(1), device_id_type=MESH)

    crossing = jnp.logical_or(r == REGIONS // 2 - 1, r == REGIONS // 2)
    neighbours = has_low.astype(jnp.int32) + has_high.astype(jnp.int32) + crossing.astype(jnp.int32)
    pl.semaphore_wait(barrier, OWNERS - 1 + neighbours)

    def own_rows(slot):
        return raw.at[slot, pl.ds(2 * m, 2), pl.ds(HALF, ROWS), :]

    def send_block(slot, peer):
        pltpu.make_async_remote_copy(
            src_ref=x.at[:, variable(slot, peer)],
            dst_ref=own_rows(slot),
            send_sem=fwd_send,
            recv_sem=fwd_recv.at[slot],
            device_id=(r, peer),
            device_id_type=MESH,
        ).start()

    def send_slot(slot, carry):
        def to_peer(step, inner):
            send_block(slot, lax.rem(m + step, OWNERS))
            return inner

        return lax.fori_loop(1, OWNERS, to_peer, carry, unroll=5)

    lax.fori_loop(0, SLOTS - 1, send_slot, 0)
    for index in range(4):

        @pl.when(m != 5 * index)
        def _(index=index):
            send_block(SLOTS - 1, 5 * index)

    def keep_slot(slot, carry):
        pltpu.make_async_copy(x.at[:, variable(slot, m)], own_rows(slot), fwd_recv.at[slot]).start()
        pltpu.make_async_copy(truth.at[variable(slot, m)], facts.at[slot], fact_sem).start()
        return carry

    lax.fori_loop(0, slots, keep_slot, 0)

    def invert(k, carry):
        cell = order[pl.ds(k, 1), :]
        row = lax.shift_right_logical(cell, 7)
        lane = jnp.bitwise_and(cell, LON - 1)
        rows_fwd[pl.ds(k, 1), :] = row
        lanes_fwd[pl.ds(k, 1), :] = lane
        at_row = lax.broadcasted_iota(jnp.int32, (ROWS, PATCH), 0) == row
        position = lax.broadcasted_iota(jnp.int32, (ROWS, PATCH), 1).astype(F32)
        patch = jnp.where(at_row, k.astype(F32), 0.0)
        place = jnp.where(at_row, position, 0.0)
        at_lane = lax.broadcasted_iota(jnp.int32, (LON, PATCH), 0) == lane
        chosen = jnp.where(at_lane, 1.0, 0.0).astype(BF16)
        return carry + dot_nt(jnp.concatenate([patch, place], axis=0).astype(BF16), chosen)

    inverse = lax.fori_loop(0, ROWS, invert, jnp.zeros((2 * ROWS, LON), F32), unroll=4)
    inverse = inverse.astype(jnp.int32)
    rows_inv[...] = inverse[:ROWS]
    lanes_inv[...] = inverse[ROWS:]

    @pl.when(slots == SLOTS)
    def _():
        pltpu.make_async_copy(facts.at[pl.ds(0, 7)], facts.at[pl.ds(0, 7)], fact_sem).wait()

    @pl.when(slots != SLOTS)
    def _():
        pltpu.make_async_copy(facts.at[pl.ds(0, 6)], facts.at[pl.ds(0, 6)], fact_sem).wait()

    for row in range(ROWS):
        fact_rows[pl.ds(row * 8, 8), :] = facts[:, row, :]

    def pick_fact(k, carry):
        picked[pl.ds(pl.multiple_of(k * 8, 8), 8), :] = pick(fact_rows, 8, rows_fwd, lanes_fwd, k)
        return carry

    lax.fori_loop(0, ROWS, pick_fact, 0, unroll=4)
    fact_rows[...] = picked[pl.ds(0, 8 * ROWS), :]

    @pl.when(jnp.logical_not(has_low))
    def _():
        def clear(slot, carry):
            raw[slot, :, pl.ds(0, HALF), :] = jnp.zeros((MEMBERS, HALF, LON), F32)
            grad[slot, :, pl.ds(0, HALF), :] = jnp.zeros((MEMBERS, HALF, LON), F32)
            return carry

        lax.fori_loop(0, slots, clear, 0)

    @pl.when(jnp.logical_not(has_high))
    def _():
        def clear(slot, carry):
            raw[slot, :, pl.ds(HALF + ROWS, HALF), :] = jnp.zeros((MEMBERS, HALF, LON), F32)
            grad[slot, :, pl.ds(HALF + ROWS, HALF), :] = jnp.zeros((MEMBERS, HALF, LON), F32)
            return carry

        lax.fori_loop(0, slots, clear, 0)

    def send_halos(field, slot, low_send, low_recv, high_send, high_recv):
        middle = field.at[slot, :, pl.ds(HALF, ROWS), :]

        @pl.when(has_high)
        def _():
            pltpu.make_async_remote_copy(
                src_ref=middle,
                dst_ref=field.at[slot, :, pl.ds(0, HALF), :],
                send_sem=high_send,
                recv_sem=high_recv.at[slot],
                device_id=above(slot),
                device_id_type=MESH,
            ).start()

        @pl.when(has_low)
        def _():
            pltpu.make_async_remote_copy(
                src_ref=middle,
                dst_ref=field.at[slot, :, pl.ds(HALF + ROWS, HALF), :],
                send_sem=low_send,
                recv_sem=low_recv.at[slot],
                device_id=below(slot),
                device_id_type=MESH,
            ).start()

    def wait_halos(field, slot, low_recv, high_recv):
        @pl.when(has_low)
        def _():
            part = field.at[slot, :, pl.ds(0, HALF), :]
            pltpu.make_async_copy(part, part, high_recv.at[slot]).wait()

        @pl.when(has_high)
        def _():
            part = field.at[slot, :, pl.ds(HALF + ROWS, HALF), :]
            pltpu.make_async_copy(part, part, low_recv.at[slot]).wait()

    def arrive(slot):
        part = raw.at[slot, :, pl.ds(HALF, ROWS), :]
        pltpu.make_async_copy(part, part, fwd_recv.at[slot]).wait()
        send_halos(raw, slot, down_send, down_recv, up_send, up_recv)

    def middle(slot):
        wait_halos(raw, slot, down_recv, up_recv)
        smooth_lat(raw.at[slot], lat, mid)
        for block in range(4):
            rows = [mid[pl.ds(block * 8 + row, MEMBERS, stride=ROWS), :] for row in range(8)]
            cells[pl.ds(block * 256, 256), :] = smooth_lon(jnp.concatenate(rows, axis=0), lon)

        def pick_patch(k, carry):
            at = pl.multiple_of(k * MEMBERS, MEMBERS)
            picked[pl.ds(at, MEMBERS), :] = pick(cells, MEMBERS, rows_fwd, lanes_fwd, k)
            return carry

        lax.fori_loop(0, ROWS, pick_patch, 0, unroll=4)

        def quad(q, carry):
            at = pl.multiple_of(q * 4 * MEMBERS, 4 * MEMBERS)
            truths = jnp.stack(
                [fact_rows[pl.ds((4 * q + i) * 8 + slot, 1), :] for i in range(4)], axis=0
            )
            cells[pl.ds(at, 4 * MEMBERS), :] = pair_block(picked[pl.ds(at, 4 * MEMBERS), :], truths)
            return carry

        lax.fori_loop(0, ROWS // 4, quad, 0, unroll=2)

        def put_row(row, carry):
            at = pl.multiple_of(row * MEMBERS, MEMBERS)
            mid[pl.ds(at, MEMBERS), :] = pick(cells, MEMBERS, rows_inv, lanes_inv, row)
            return carry

        lax.fori_loop(0, ROWS, put_row, 0, unroll=4)
        for member in range(MEMBERS):
            grad[slot, member, pl.ds(HALF, ROWS), :] = mid[pl.ds(member, ROWS, stride=MEMBERS), :]

    def finish(slot):
        wait_halos(grad, slot, down2_recv, up2_recv)
        smooth_lat(grad.at[slot], lat, mid)
        for block in range(4):
            part = smooth_lon(mid[pl.ds(block * 256, 256), :], lon)
            done[slot, pl.ds(block * 8, 8)] = part.reshape(8, ROWS, LON)

    def give_back(slot):
        def to_peer(step, carry):
            peer = lax.rem(m + step, OWNERS)
            pltpu.make_async_remote_copy(
                src_ref=done.at[slot, pl.ds(2 * peer, 2)],
                dst_ref=out.at[:, variable(slot, m)],
                send_sem=ret_send,
                recv_sem=ret_recv,
                device_id=(r, peer),
                device_id_type=MESH,
            ).start()
            return carry

        lax.fori_loop(1, OWNERS, to_peer, 0, unroll=5)
        pltpu.make_async_copy(
            done.at[slot, pl.ds(2 * m, 2)], out.at[:, variable(slot, m)], ret_recv
        ).start()

    def step(i, carry):
        @pl.when(jnp.logical_and(i >= 5, i < slots + 5))
        def _():
            give_back(i - 5)

        @pl.when(i < slots)
        def _():
            arrive(i)

        @pl.when(jnp.logical_and(i >= 2, i < slots + 2))
        def _():
            middle(i - 2)

        @pl.when(jnp.logical_and(i >= 4, i < slots + 4))
        def _():
            finish(i - 4)

        @pl.when(jnp.logical_and(i >= 2, i < slots + 2))
        def _():
            send_halos(grad, i - 2, down2_send, down2_recv, up2_send, up2_recv)

        return carry

    lax.fori_loop(0, SLOTS + 5, step, 0)

    def drain(count):
        pltpu.make_async_copy(
            x.at[:, pl.ds(0, V - count)], x.at[:, pl.ds(0, V - count)], fwd_send
        ).wait()
        sent = done.at[pl.ds(0, count), pl.ds(0, 2 * OWNERS - 2)]
        pltpu.make_async_copy(sent, sent, ret_send).wait()

        @pl.when(has_high)
        def _():
            for field, sem in ((raw, up_send), (grad, up2_send)):
                part = field.at[pl.ds(0, count), :, pl.ds(HALF, ROWS), :]
                pltpu.make_async_copy(part, part, sem).wait()

        @pl.when(has_low)
        def _():
            for field, sem in ((raw, down_send), (grad, down2_send)):
                part = field.at[pl.ds(0, count), :, pl.ds(HALF, ROWS), :]
                pltpu.make_async_copy(part, part, sem).wait()

    @pl.when(slots == SLOTS)
    def _():
        drain(SLOTS)

    @pl.when(slots != SLOTS)
    def _():
        drain(SLOTS - 1)

    pltpu.make_async_copy(out, out, ret_recv).wait()


def on_device(predicted_states, observed_analysis, tile_location_sequence):
    order = tile_location_sequence.reshape(ROWS, PATCH)
    dma = pltpu.SemaphoreType.DMA
    vmem = pl.BlockSpec(memory_space=pltpu.VMEM)
    hbm = pl.BlockSpec(memory_space=pl.ANY)
    return pl.pallas_call(
        kernel,
        out_shape=jax.ShapeDtypeStruct((2, V, ROWS, LON), F32),
        in_specs=[hbm, hbm, vmem, vmem, vmem],
        out_specs=hbm,
        scratch_shapes=[
            pltpu.VMEM((SLOTS, MEMBERS, SPAN, LON), F32),
            pltpu.VMEM((SLOTS, MEMBERS, SPAN, LON), F32),
            pltpu.VMEM((SLOTS, MEMBERS, ROWS, LON), F32),
            pltpu.VMEM((MEMBERS * ROWS, LON), F32),
            pltpu.VMEM((MEMBERS * ROWS, LON), F32),
            pltpu.VMEM((MEMBERS * ROWS, LON), F32),
            pltpu.VMEM((8, ROWS, LON), F32),
            pltpu.VMEM((8 * ROWS, LON), F32),
            pltpu.VMEM((ROWS, LON), jnp.int32),
            pltpu.VMEM((ROWS, LON), jnp.int32),
            pltpu.VMEM((ROWS, LON), jnp.int32),
            pltpu.VMEM((ROWS, LON), jnp.int32),
            dma(()), dma((SLOTS,)), dma(()), dma((SLOTS,)), dma(()), dma((SLOTS,)),
            dma(()), dma((SLOTS,)), dma(()), dma((SLOTS,)), dma(()), dma(()), dma(()),
        ],
        compiler_params=pltpu.CompilerParams(
            collective_id=0, has_side_effects=True, vmem_limit_bytes=56 * 1024 * 1024
        ),
    )(
        predicted_states,
        observed_analysis,
        order,
        jnp.asarray(lat_weights()),
        jnp.asarray(lon_weights()),
    )


def solution(mesh):
    in_specs = (P("member", None, "region", None), P(None, "region", None), P("region", None))
    out_specs = P("member", None, "region", None)
    return jax.shard_map(
        on_device, mesh=mesh, in_specs=in_specs, out_specs=out_specs, check_vma=False
    )
```

```python
import math

import jax
import jax.numpy as jnp
import numpy as np
from jax import lax
from jax.experimental import pallas as pl
from jax.experimental.pallas import tpu as pltpu
from jax.sharding import PartitionSpec as P

V = 100
ROWS = 32
LON = 128
HALF = 32
PATCH = 128
MEMBERS = 32
OWNERS = 16
REGIONS = 16
SLOTS = 7
SPAN = ROWS + 2 * HALF
CELLS = ROWS * LON
MESH = pl.DeviceIdType.MESH
F32 = jnp.float32
BF16 = jnp.bfloat16


def kernel_values(offset):
    sigma = HALF / 2.0
    steps = np.arange(-HALF, HALF + 1).astype(np.float64)
    norm = np.sum(np.exp(-(steps * steps) / (2.0 * sigma * sigma)))
    bell = np.exp(-(offset * offset) / (2.0 * sigma * sigma)) / norm
    value = 0.5 * (offset == 0.0) + 0.5 * bell
    return np.where(np.abs(offset) <= HALF, value, 0.0).astype(np.float32)


def halves(values):
    high = values.astype(BF16)
    low = (values - high.astype(np.float32)).astype(BF16)
    return high, low


def lat_weights():
    rows = np.arange(ROWS)[:, None]
    span = np.arange(SPAN)[None, :]
    high, low = halves(kernel_values((span - HALF - rows).astype(np.float64)))
    return np.concatenate(
        [np.concatenate([high, high], 1), np.concatenate([low, np.zeros_like(low)], 1)], 0
    )


def lon_weights():
    first = np.arange(LON)[:, None]
    second = np.arange(LON)[None, :]
    high, low = halves(kernel_values((second - first).astype(np.float64)))
    return np.concatenate(
        [np.concatenate([high, low], 1), np.concatenate([high, np.zeros_like(low)], 1)], 0
    )


def split(values):
    high = values.astype(BF16)
    low = (values - high.astype(F32)).astype(BF16)
    return high, low


def dot(a, b):
    return lax.dot_general(a, b, (((1,), (0,)), ((), ())), preferred_element_type=F32)


def dot_nt(a, b):
    return lax.dot_general(a, b, (((1,), (1,)), ((), ())), preferred_element_type=F32)


LANES = lax.GatherDimensionNumbers(
    offset_dims=(),
    collapsed_slice_dims=(1,),
    start_index_map=(1,),
    operand_batching_dims=(0,),
    start_indices_batching_dims=(0,),
)


def take_lanes(values, lanes):
    return lax.gather(
        values,
        lanes[..., None],
        LANES,
        slice_sizes=(1, 1),
        mode=lax.GatherScatterMode.PROMISE_IN_BOUNDS,
    )


def pick(src, group, row_of, lane_of, index):
    lanes = jnp.broadcast_to(lane_of[pl.ds(index, 1), :], (group, LON))
    rows = jnp.broadcast_to(row_of[pl.ds(index, 1), :], (group, LON))
    total = jnp.zeros((group, LON), F32)
    for row in range(ROWS):
        found = take_lanes(src[pl.ds(row * group, group), :], lanes)
        total = jnp.where(rows == row, found, total)
    return total


def smooth_lat(field, lat, mid):
    def pair(index, carry):
        both = jnp.concatenate([field[2 * index], field[2 * index + 1]], axis=1)
        high, low = split(both)
        parts = dot(lat[...], jnp.concatenate([high, low], axis=0))
        rows = parts[:ROWS] + parts[ROWS:]
        mid[pl.ds(pl.multiple_of(2 * index * ROWS, 64), ROWS), :] = rows[:, :LON]
        mid[pl.ds(pl.multiple_of(2 * index * ROWS + ROWS, 32), ROWS), :] = rows[:, LON:]
        return carry

    lax.fori_loop(0, MEMBERS // 2, pair, 0, unroll=2)


def smooth_lon(block, lon):
    high, low = split(block)
    parts = dot(jnp.concatenate([high, low], axis=1), lon[...])
    return parts[:, :LON] + parts[:, LON:]


def pair_block(a, truths):
    count = 4
    cube = a.reshape(count, MEMBERS, PATCH)
    mean = jnp.sum(cube, axis=1, keepdims=True) * (1.0 / MEMBERS)
    e = (cube - mean).reshape(count * MEMBERS, PATCH)
    d = (cube - truths).reshape(count * MEMBERS, PATCH)
    toward = d * lax.rsqrt(jnp.sum(d * d, axis=1, keepdims=True) + 1e-06)
    size = count * MEMBERS
    left = lax.broadcasted_iota(jnp.int32, (size, size), 0)
    right = lax.broadcasted_iota(jnp.int32, (size, size), 1)
    same = left == right
    other = jnp.logical_and(lax.div(left, MEMBERS) == lax.div(right, MEMBERS), left != right)
    high, low = split(e)
    gram = dot_nt(jnp.concatenate([high, low], axis=1), jnp.concatenate([high, high], axis=1))
    gram = gram + dot_nt(high, low)
    diagonal = jnp.where(same, gram, 0.0)
    dist = jnp.sum(diagonal, axis=1, keepdims=True) + jnp.sum(diagonal, axis=0, keepdims=True)
    dist = jnp.maximum(dist - 2.0 * gram, 0.0)
    weights = jnp.where(other, lax.rsqrt(dist + 1e-06), 0.0)
    pulled = jnp.sum(weights, axis=1, keepdims=True)
    mixing = jnp.where(same, pulled, -weights)
    mix_high, mix_low = split(mixing)
    apart = dot(jnp.concatenate([mix_high, mix_low], axis=1), jnp.concatenate([high, high], axis=0))
    apart = apart + dot(mix_high, low)
    return math.sqrt(PATCH) * (toward - apart * (1.0 / MEMBERS))


def kernel(
    x, truth, order, lat, lon, out,
    raw, grad, done, mid, cells, picked, facts, fact_rows, rows_fwd, lanes_fwd, rows_inv, lanes_inv,
    fwd_send, fwd_recv, up_send, up_recv, down_send, down_recv,
    up2_send, up2_recv, down2_send, down2_recv, ret_send, ret_recv, fact_sem,
):
    r = lax.axis_index("region")
    m = lax.axis_index("member")
    slots = jnp.where(lax.rem(m, 5) == 0, SLOTS, SLOTS - 1)
    has_low = r > 0
    has_high = r < REGIONS - 1

    def turned(owner, by):
        return lax.div(owner, 4) * 4 + lax.rem(owner + 4 + by, 4)

    def variable(slot, owner):
        back = jnp.logical_and(lax.rem(slot, 2) == 1, r >= REGIONS // 2)
        place = jnp.where(back, turned(owner, 1), owner)
        return jnp.where(slot == SLOTS - 1, 96 + lax.div(owner, 5), slot * OWNERS + place)

    def above(slot):
        cross = jnp.logical_and(lax.rem(slot, 2) == 1, r == REGIONS // 2 - 1)
        return (r + 1, jnp.where(cross, turned(m, -1), m))

    def below(slot):
        cross = jnp.logical_and(lax.rem(slot, 2) == 1, r == REGIONS // 2)
        return (r - 1, jnp.where(cross, turned(m, 1), m))

    barrier = pltpu.get_barrier_semaphore()
    for step in range(1, OWNERS):
        peer = (r, lax.rem(m + step, OWNERS))
        pl.semaphore_signal(barrier, inc=1, device_id=peer, device_id_type=MESH)

    @pl.when(has_low)
    def _():
        pl.semaphore_signal(barrier, inc=1, device_id=(r - 1, m), device_id_type=MESH)

    @pl.when(has_high)
    def _():
        pl.semaphore_signal(barrier, inc=1, device_id=(r + 1, m), device_id_type=MESH)

    @pl.when(r == REGIONS // 2 - 1)
    def _():
        pl.semaphore_signal(barrier, inc=1, device_id=above(1), device_id_type=MESH)

    @pl.when(r == REGIONS // 2)
    def _():
        pl.semaphore_signal(barrier, inc=1, device_id=below(1), device_id_type=MESH)

    crossing = jnp.logical_or(r == REGIONS // 2 - 1, r == REGIONS // 2)
    neighbours = has_low.astype(jnp.int32) + has_high.astype(jnp.int32) + crossing.astype(jnp.int32)
    pl.semaphore_wait(barrier, OWNERS - 1 + neighbours)

    def own_rows(slot):
        return raw.at[slot, pl.ds(2 * m, 2), pl.ds(HALF, ROWS), :]

    def send_block(slot, peer):
        pltpu.make_async_remote_copy(
            src_ref=x.at[:, variable(slot, peer)],
            dst_ref=own_rows(slot),
            send_sem=fwd_send,
            recv_sem=fwd_recv.at[slot],
            device_id=(r, peer),
            device_id_type=MESH,
        ).start()

    def send_slot(slot, carry):
        def to_peer(step, inner):
            send_block(slot, lax.rem(m + step, OWNERS))
            return inner

        return lax.fori_loop(1, OWNERS, to_peer, carry, unroll=5)

    lax.fori_loop(0, 1, send_slot, 0)

    def send_slots_tail():
        for index in range(4):

            @pl.when(m != 5 * index)
            def _(index=index):
                send_block(SLOTS - 1, 5 * index)

    def keep_slot(slot, carry):
        pltpu.make_async_copy(x.at[:, variable(slot, m)], own_rows(slot), fwd_recv.at[slot]).start()
        pltpu.make_async_copy(truth.at[variable(slot, m)], facts.at[slot], fact_sem).start()
        return carry

    lax.fori_loop(0, slots, keep_slot, 0)

    def invert(k, carry):
        cell = order[pl.ds(k, 1), :]
        row = lax.shift_right_logical(cell, 7)
        lane = jnp.bitwise_and(cell, LON - 1)
        rows_fwd[pl.ds(k, 1), :] = row
        lanes_fwd[pl.ds(k, 1), :] = lane
        at_row = lax.broadcasted_iota(jnp.int32, (ROWS, PATCH), 0) == row
        position = lax.broadcasted_iota(jnp.int32, (ROWS, PATCH), 1).astype(F32)
        patch = jnp.where(at_row, k.astype(F32), 0.0)
        place = jnp.where(at_row, position, 0.0)
        at_lane = lax.broadcasted_iota(jnp.int32, (LON, PATCH), 0) == lane
        chosen = jnp.where(at_lane, 1.0, 0.0).astype(BF16)
        return carry + dot_nt(jnp.concatenate([patch, place], axis=0).astype(BF16), chosen)

    inverse = lax.fori_loop(0, ROWS, invert, jnp.zeros((2 * ROWS, LON), F32), unroll=4)
    inverse = inverse.astype(jnp.int32)
    rows_inv[...] = inverse[:ROWS]
    lanes_inv[...] = inverse[ROWS:]

    @pl.when(slots == SLOTS)
    def _():
        pltpu.make_async_copy(facts.at[pl.ds(0, 7)], facts.at[pl.ds(0, 7)], fact_sem).wait()

    @pl.when(slots != SLOTS)
    def _():
        pltpu.make_async_copy(facts.at[pl.ds(0, 6)], facts.at[pl.ds(0, 6)], fact_sem).wait()

    for row in range(ROWS):
        fact_rows[pl.ds(row * 8, 8), :] = facts[:, row, :]

    def pick_fact(k, carry):
        picked[pl.ds(pl.multiple_of(k * 8, 8), 8), :] = pick(fact_rows, 8, rows_fwd, lanes_fwd, k)
        return carry

    lax.fori_loop(0, ROWS, pick_fact, 0, unroll=4)
    fact_rows[...] = picked[pl.ds(0, 8 * ROWS), :]

    @pl.when(jnp.logical_not(has_low))
    def _():
        def clear(slot, carry):
            raw[slot, :, pl.ds(0, HALF), :] = jnp.zeros((MEMBERS, HALF, LON), F32)
            grad[slot, :, pl.ds(0, HALF), :] = jnp.zeros((MEMBERS, HALF, LON), F32)
            return carry

        lax.fori_loop(0, slots, clear, 0)

    @pl.when(jnp.logical_not(has_high))
    def _():
        def clear(slot, carry):
            raw[slot, :, pl.ds(HALF + ROWS, HALF), :] = jnp.zeros((MEMBERS, HALF, LON), F32)
            grad[slot, :, pl.ds(HALF + ROWS, HALF), :] = jnp.zeros((MEMBERS, HALF, LON), F32)
            return carry

        lax.fori_loop(0, slots, clear, 0)

    def send_halos(field, slot, low_send, low_recv, high_send, high_recv):
        middle = field.at[slot, :, pl.ds(HALF, ROWS), :]

        @pl.when(has_high)
        def _():
            pltpu.make_async_remote_copy(
                src_ref=middle,
                dst_ref=field.at[slot, :, pl.ds(0, HALF), :],
                send_sem=high_send,
                recv_sem=high_recv.at[slot],
                device_id=above(slot),
                device_id_type=MESH,
            ).start()

        @pl.when(has_low)
        def _():
            pltpu.make_async_remote_copy(
                src_ref=middle,
                dst_ref=field.at[slot, :, pl.ds(HALF + ROWS, HALF), :],
                send_sem=low_send,
                recv_sem=low_recv.at[slot],
                device_id=below(slot),
                device_id_type=MESH,
            ).start()

    def wait_halos(field, slot, low_recv, high_recv):
        @pl.when(has_low)
        def _():
            part = field.at[slot, :, pl.ds(0, HALF), :]
            pltpu.make_async_copy(part, part, high_recv.at[slot]).wait()

        @pl.when(has_high)
        def _():
            part = field.at[slot, :, pl.ds(HALF + ROWS, HALF), :]
            pltpu.make_async_copy(part, part, low_recv.at[slot]).wait()

    def arrive(slot):
        part = raw.at[slot, :, pl.ds(HALF, ROWS), :]
        pltpu.make_async_copy(part, part, fwd_recv.at[slot]).wait()
        send_halos(raw, slot, down_send, down_recv, up_send, up_recv)

    def middle(slot):
        wait_halos(raw, slot, down_recv, up_recv)
        smooth_lat(raw.at[slot], lat, mid)
        for block in range(4):
            rows = [mid[pl.ds(block * 8 + row, MEMBERS, stride=ROWS), :] for row in range(8)]
            cells[pl.ds(block * 256, 256), :] = smooth_lon(jnp.concatenate(rows, axis=0), lon)

        def pick_patch(k, carry):
            at = pl.multiple_of(k * MEMBERS, MEMBERS)
            picked[pl.ds(at, MEMBERS), :] = pick(cells, MEMBERS, rows_fwd, lanes_fwd, k)
            return carry

        lax.fori_loop(0, ROWS, pick_patch, 0, unroll=4)

        def quad(q, carry):
            at = pl.multiple_of(q * 4 * MEMBERS, 4 * MEMBERS)
            truths = jnp.stack(
                [fact_rows[pl.ds((4 * q + i) * 8 + slot, 1), :] for i in range(4)], axis=0
            )
            cells[pl.ds(at, 4 * MEMBERS), :] = pair_block(picked[pl.ds(at, 4 * MEMBERS), :], truths)
            return carry

        lax.fori_loop(0, ROWS // 4, quad, 0, unroll=2)

        def put_row(row, carry):
            at = pl.multiple_of(row * MEMBERS, MEMBERS)
            mid[pl.ds(at, MEMBERS), :] = pick(cells, MEMBERS, rows_inv, lanes_inv, row)
            return carry

        lax.fori_loop(0, ROWS, put_row, 0, unroll=4)
        for member in range(MEMBERS):
            grad[slot, member, pl.ds(HALF, ROWS), :] = mid[pl.ds(member, ROWS, stride=MEMBERS), :]

    def finish(slot):
        wait_halos(grad, slot, down2_recv, up2_recv)
        smooth_lat(grad.at[slot], lat, mid)
        for block in range(4):
            part = smooth_lon(mid[pl.ds(block * 256, 256), :], lon)
            done[slot, pl.ds(block * 8, 8)] = part.reshape(8, ROWS, LON)

    def give_back(slot):
        def to_peer(step, carry):
            peer = lax.rem(m + step, OWNERS)
            pltpu.make_async_remote_copy(
                src_ref=done.at[slot, pl.ds(2 * peer, 2)],
                dst_ref=out.at[:, variable(slot, m)],
                send_sem=ret_send,
                recv_sem=ret_recv,
                device_id=(r, peer),
                device_id_type=MESH,
            ).start()
            return carry

        lax.fori_loop(1, OWNERS, to_peer, 0, unroll=5)
        pltpu.make_async_copy(
            done.at[slot, pl.ds(2 * m, 2)], out.at[:, variable(slot, m)], ret_recv
        ).start()

    def step(i, carry):
        @pl.when(i + 1 < SLOTS - 1)
        def _():
            send_slot(i + 1, 0)

        @pl.when(i + 1 == SLOTS - 1)
        def _():
            send_slots_tail()

        @pl.when(jnp.logical_and(i >= 5, i < slots + 5))
        def _():
            give_back(i - 5)

        @pl.when(i < slots)
        def _():
            arrive(i)

        @pl.when(jnp.logical_and(i >= 2, i < slots + 2))
        def _():
            middle(i - 2)

        @pl.when(jnp.logical_and(i >= 4, i < slots + 4))
        def _():
            finish(i - 4)

        @pl.when(jnp.logical_and(i >= 2, i < slots + 2))
        def _():
            send_halos(grad, i - 2, down2_send, down2_recv, up2_send, up2_recv)

        return carry

    lax.fori_loop(0, SLOTS + 5, step, 0)

    def drain(count):
        pltpu.make_async_copy(
            x.at[:, pl.ds(0, V - count)], x.at[:, pl.ds(0, V - count)], fwd_send
        ).wait()
        sent = done.at[pl.ds(0, count), pl.ds(0, 2 * OWNERS - 2)]
        pltpu.make_async_copy(sent, sent, ret_send).wait()

        @pl.when(has_high)
        def _():
            for field, sem in ((raw, up_send), (grad, up2_send)):
                part = field.at[pl.ds(0, count), :, pl.ds(HALF, ROWS), :]
                pltpu.make_async_copy(part, part, sem).wait()

        @pl.when(has_low)
        def _():
            for field, sem in ((raw, down_send), (grad, down2_send)):
                part = field.at[pl.ds(0, count), :, pl.ds(HALF, ROWS), :]
                pltpu.make_async_copy(part, part, sem).wait()

    @pl.when(slots == SLOTS)
    def _():
        drain(SLOTS)

    @pl.when(slots != SLOTS)
    def _():
        drain(SLOTS - 1)

    pltpu.make_async_copy(out, out, ret_recv).wait()


def on_device(predicted_states, observed_analysis, tile_location_sequence):
    order = tile_location_sequence.reshape(ROWS, PATCH)
    dma = pltpu.SemaphoreType.DMA
    vmem = pl.BlockSpec(memory_space=pltpu.VMEM)
    hbm = pl.BlockSpec(memory_space=pl.ANY)
    return pl.pallas_call(
        kernel,
        out_shape=jax.ShapeDtypeStruct((2, V, ROWS, LON), F32),
        in_specs=[hbm, hbm, vmem, vmem, vmem],
        out_specs=hbm,
        scratch_shapes=[
            pltpu.VMEM((SLOTS, MEMBERS, SPAN, LON), F32),
            pltpu.VMEM((SLOTS, MEMBERS, SPAN, LON), F32),
            pltpu.VMEM((SLOTS, MEMBERS, ROWS, LON), F32),
            pltpu.VMEM((MEMBERS * ROWS, LON), F32),
            pltpu.VMEM((MEMBERS * ROWS, LON), F32),
            pltpu.VMEM((MEMBERS * ROWS, LON), F32),
            pltpu.VMEM((8, ROWS, LON), F32),
            pltpu.VMEM((8 * ROWS, LON), F32),
            pltpu.VMEM((ROWS, LON), jnp.int32),
            pltpu.VMEM((ROWS, LON), jnp.int32),
            pltpu.VMEM((ROWS, LON), jnp.int32),
            pltpu.VMEM((ROWS, LON), jnp.int32),
            dma(()), dma((SLOTS,)), dma(()), dma((SLOTS,)), dma(()), dma((SLOTS,)),
            dma(()), dma((SLOTS,)), dma(()), dma((SLOTS,)), dma(()), dma(()), dma(()),
        ],
        compiler_params=pltpu.CompilerParams(
            collective_id=0, has_side_effects=True, vmem_limit_bytes=56 * 1024 * 1024
        ),
    )(
        predicted_states,
        observed_analysis,
        order,
        jnp.asarray(lat_weights()),
        jnp.asarray(lon_weights()),
    )


def solution(mesh):
    in_specs = (P("member", None, "region", None), P(None, "region", None), P("region", None))
    out_specs = P("member", None, "region", None)
    return jax.shard_map(
        on_device, mesh=mesh, in_specs=in_specs, out_specs=out_specs, check_vma=False
    )
```

```python
import math

import jax
import jax.numpy as jnp
import numpy as np
from jax import lax
from jax.experimental import pallas as pl
from jax.experimental.pallas import tpu as pltpu
from jax.sharding import PartitionSpec as P

V = 100
ROWS = 32
LON = 128
HALF = 32
PATCH = 128
MEMBERS = 32
OWNERS = 16
REGIONS = 16
SLOTS = 7
SPAN = ROWS + 2 * HALF
CELLS = ROWS * LON
TOP = REGIONS // 2 - 1
UP_RELAYS = (4, 2)
DOWN_RELAYS = (11, 13)
RELAYS = 2
AWAY = 0
PIECE = 10
STRAIGHT = MEMBERS - RELAYS * PIECE
MESH = pl.DeviceIdType.MESH
F32 = jnp.float32
BF16 = jnp.bfloat16


def kernel_values(offset):
    sigma = HALF / 2.0
    steps = np.arange(-HALF, HALF + 1).astype(np.float64)
    norm = np.sum(np.exp(-(steps * steps) / (2.0 * sigma * sigma)))
    bell = np.exp(-(offset * offset) / (2.0 * sigma * sigma)) / norm
    value = 0.5 * (offset == 0.0) + 0.5 * bell
    return np.where(np.abs(offset) <= HALF, value, 0.0).astype(np.float32)


def halves(values):
    high = values.astype(BF16)
    low = (values - high.astype(np.float32)).astype(BF16)
    return high, low


def lat_weights():
    rows = np.arange(ROWS)[:, None]
    span = np.arange(SPAN)[None, :]
    high, low = halves(kernel_values((span - HALF - rows).astype(np.float64)))
    return np.concatenate(
        [np.concatenate([high, high], 1), np.concatenate([low, np.zeros_like(low)], 1)], 0
    )


def lon_weights():
    first = np.arange(LON)[:, None]
    second = np.arange(LON)[None, :]
    high, low = halves(kernel_values((second - first).astype(np.float64)))
    return np.concatenate(
        [np.concatenate([high, low], 1), np.concatenate([high, np.zeros_like(low)], 1)], 0
    )


def split(values):
    high = values.astype(BF16)
    low = (values - high.astype(F32)).astype(BF16)
    return high, low


def dot(a, b):
    return lax.dot_general(a, b, (((1,), (0,)), ((), ())), preferred_element_type=F32)


def dot_nt(a, b):
    return lax.dot_general(a, b, (((1,), (1,)), ((), ())), preferred_element_type=F32)


LANES = lax.GatherDimensionNumbers(
    offset_dims=(),
    collapsed_slice_dims=(1,),
    start_index_map=(1,),
    operand_batching_dims=(0,),
    start_indices_batching_dims=(0,),
)


def take_lanes(values, lanes):
    return lax.gather(
        values,
        lanes[..., None],
        LANES,
        slice_sizes=(1, 1),
        mode=lax.GatherScatterMode.PROMISE_IN_BOUNDS,
    )


def pick(src, group, row_of, lane_of, index):
    lanes = jnp.broadcast_to(lane_of[pl.ds(index, 1), :], (group, LON))
    rows = jnp.broadcast_to(row_of[pl.ds(index, 1), :], (group, LON))
    total = jnp.zeros((group, LON), F32)
    for row in range(ROWS):
        found = take_lanes(src[pl.ds(row * group, group), :], lanes)
        total = jnp.where(rows == row, found, total)
    return total


def smooth_lat(field, lat, mid):
    def pair(index, carry):
        both = jnp.concatenate([field[2 * index], field[2 * index + 1]], axis=1)
        high, low = split(both)
        parts = dot(lat[...], jnp.concatenate([high, low], axis=0))
        rows = parts[:ROWS] + parts[ROWS:]
        mid[pl.ds(pl.multiple_of(2 * index * ROWS, 64), ROWS), :] = rows[:, :LON]
        mid[pl.ds(pl.multiple_of(2 * index * ROWS + ROWS, 32), ROWS), :] = rows[:, LON:]
        return carry

    lax.fori_loop(0, MEMBERS // 2, pair, 0, unroll=2)


def smooth_lon(block, lon):
    high, low = split(block)
    parts = dot(jnp.concatenate([high, low], axis=1), lon[...])
    return parts[:, :LON] + parts[:, LON:]


def pair_block(a, truths):
    count = 4
    cube = a.reshape(count, MEMBERS, PATCH)
    mean = jnp.sum(cube, axis=1, keepdims=True) * (1.0 / MEMBERS)
    e = (cube - mean).reshape(count * MEMBERS, PATCH)
    d = (cube - truths).reshape(count * MEMBERS, PATCH)
    toward = d * lax.rsqrt(jnp.sum(d * d, axis=1, keepdims=True) + 1e-06)
    size = count * MEMBERS
    left = lax.broadcasted_iota(jnp.int32, (size, size), 0)
    right = lax.broadcasted_iota(jnp.int32, (size, size), 1)
    same = left == right
    other = jnp.logical_and(lax.div(left, MEMBERS) == lax.div(right, MEMBERS), left != right)
    high, low = split(e)
    gram = dot_nt(jnp.concatenate([high, low], axis=1), jnp.concatenate([high, high], axis=1))
    gram = gram + dot_nt(high, low)
    diagonal = jnp.where(same, gram, 0.0)
    dist = jnp.sum(diagonal, axis=1, keepdims=True) + jnp.sum(diagonal, axis=0, keepdims=True)
    dist = jnp.maximum(dist - 2.0 * gram, 0.0)
    weights = jnp.where(other, lax.rsqrt(dist + 1e-06), 0.0)
    pulled = jnp.sum(weights, axis=1, keepdims=True)
    mixing = jnp.where(same, pulled, -weights)
    mix_high, mix_low = split(mixing)
    apart = dot(jnp.concatenate([mix_high, mix_low], axis=1), jnp.concatenate([high, high], axis=0))
    apart = apart + dot(mix_high, low)
    return math.sqrt(PATCH) * (toward - apart * (1.0 / MEMBERS))


def kernel(
    x, truth, order, lat, lon, out,
    raw, grad, done, mid, cells, picked, facts, fact_rows, rows_fwd, lanes_fwd, rows_inv, lanes_inv,
    fwd_send, fwd_recv, up_send, up_recv, down_send, down_recv,
    up2_send, up2_recv, down2_send, down2_recv, ret_send, ret_recv, fact_sem,
    way, way2, way_send, way_recv, way2_send, way2_recv,
):
    r = lax.axis_index("region")
    m = lax.axis_index("member")
    slots = jnp.where(lax.rem(m, 5) == 0, SLOTS, SLOTS - 1)
    has_low = r > 0
    has_high = r < REGIONS - 1

    def turned(owner, by):
        return lax.div(owner, 4) * 4 + lax.rem(owner + 4 + by, 4)

    def variable(slot, owner):
        back = jnp.logical_and(lax.rem(slot, 2) == 1, r >= REGIONS // 2)
        place = jnp.where(back, turned(owner, 1), owner)
        return jnp.where(slot == SLOTS - 1, 96 + lax.div(owner, 5), slot * OWNERS + place)

    def above(slot):
        cross = jnp.logical_and(lax.rem(slot, 2) == 1, r == REGIONS // 2 - 1)
        return (r + 1, jnp.where(cross, turned(m, -1), m))

    def below(slot):
        cross = jnp.logical_and(lax.rem(slot, 2) == 1, r == REGIONS // 2)
        return (r - 1, jnp.where(cross, turned(m, 1), m))

    barrier = pltpu.get_barrier_semaphore()
    for step in range(1, OWNERS):
        peer = (r, lax.rem(m + step, OWNERS))
        pl.semaphore_signal(barrier, inc=1, device_id=peer, device_id_type=MESH)

    @pl.when(has_low)
    def _():
        pl.semaphore_signal(barrier, inc=1, device_id=(r - 1, m), device_id_type=MESH)

    @pl.when(has_high)
    def _():
        pl.semaphore_signal(barrier, inc=1, device_id=(r + 1, m), device_id_type=MESH)

    relay_up = jnp.logical_or(r == UP_RELAYS[0], r == UP_RELAYS[1])
    relay_down = jnp.logical_or(r == DOWN_RELAYS[0], r == DOWN_RELAYS[1])
    at_top = r == TOP
    at_bottom = r == TOP + 1
    ahead = turned(m, 1)
    behind = turned(m, -1)

    def greet(condition, peers):
        @pl.when(condition)
        def _():
            for peer in peers:
                pl.semaphore_signal(barrier, inc=1, device_id=peer, device_id_type=MESH)

        return condition.astype(jnp.int32) * len(peers)

    greeted = has_low.astype(jnp.int32) + has_high.astype(jnp.int32)
    greeted += greet(
        at_top,
        [(TOP + 1, behind)]
        + [(region, m) for region in UP_RELAYS]
        + [(region, who) for region in DOWN_RELAYS for who in (m, behind)],
    )
    greeted += greet(
        at_bottom,
        [(TOP, ahead)]
        + [(region, m) for region in DOWN_RELAYS]
        + [(region, who) for region in UP_RELAYS for who in (m, ahead)],
    )
    greeted += greet(relay_up, [(TOP, m), (TOP + 1, m), (TOP + 1, behind)])
    greeted += greet(relay_down, [(TOP + 1, m), (TOP, m), (TOP, ahead)])
    pl.semaphore_wait(barrier, OWNERS - 1 + greeted)

    def own_rows(slot):
        return raw.at[slot, pl.ds(2 * m, 2), pl.ds(HALF, ROWS), :]

    def send_block(slot, peer):
        pltpu.make_async_remote_copy(
            src_ref=x.at[:, variable(slot, peer)],
            dst_ref=own_rows(slot),
            send_sem=fwd_send,
            recv_sem=fwd_recv.at[slot],
            device_id=(r, peer),
            device_id_type=MESH,
        ).start()

    def send_slot(slot, carry):
        def to_peer(step, inner):
            send_block(slot, lax.rem(m + step, OWNERS))
            return inner

        return lax.fori_loop(1, OWNERS, to_peer, carry, unroll=5)

    lax.fori_loop(0, 1, send_slot, 0)

    def send_slots_tail():
        for index in range(4):

            @pl.when(m != 5 * index)
            def _(index=index):
                send_block(SLOTS - 1, 5 * index)

    def keep_slot(slot, carry):
        pltpu.make_async_copy(x.at[:, variable(slot, m)], own_rows(slot), fwd_recv.at[slot]).start()
        pltpu.make_async_copy(truth.at[variable(slot, m)], facts.at[slot], fact_sem).start()
        return carry

    lax.fori_loop(0, slots, keep_slot, 0)

    def invert(k, carry):
        cell = order[pl.ds(k, 1), :]
        row = lax.shift_right_logical(cell, 7)
        lane = jnp.bitwise_and(cell, LON - 1)
        rows_fwd[pl.ds(k, 1), :] = row
        lanes_fwd[pl.ds(k, 1), :] = lane
        at_row = lax.broadcasted_iota(jnp.int32, (ROWS, PATCH), 0) == row
        position = lax.broadcasted_iota(jnp.int32, (ROWS, PATCH), 1).astype(F32)
        patch = jnp.where(at_row, k.astype(F32), 0.0)
        place = jnp.where(at_row, position, 0.0)
        at_lane = lax.broadcasted_iota(jnp.int32, (LON, PATCH), 0) == lane
        chosen = jnp.where(at_lane, 1.0, 0.0).astype(BF16)
        return carry + dot_nt(jnp.concatenate([patch, place], axis=0).astype(BF16), chosen)

    inverse = lax.fori_loop(0, ROWS, invert, jnp.zeros((2 * ROWS, LON), F32), unroll=4)
    inverse = inverse.astype(jnp.int32)
    rows_inv[...] = inverse[:ROWS]
    lanes_inv[...] = inverse[ROWS:]

    @pl.when(slots == SLOTS)
    def _():
        pltpu.make_async_copy(facts.at[pl.ds(0, 7)], facts.at[pl.ds(0, 7)], fact_sem).wait()

    @pl.when(slots != SLOTS)
    def _():
        pltpu.make_async_copy(facts.at[pl.ds(0, 6)], facts.at[pl.ds(0, 6)], fact_sem).wait()

    for row in range(ROWS):
        fact_rows[pl.ds(row * 8, 8), :] = facts[:, row, :]

    def pick_fact(k, carry):
        picked[pl.ds(pl.multiple_of(k * 8, 8), 8), :] = pick(fact_rows, 8, rows_fwd, lanes_fwd, k)
        return carry

    lax.fori_loop(0, ROWS, pick_fact, 0, unroll=4)
    fact_rows[...] = picked[pl.ds(0, 8 * ROWS), :]

    @pl.when(jnp.logical_not(has_low))
    def _():
        def clear(slot, carry):
            raw[slot, :, pl.ds(0, HALF), :] = jnp.zeros((MEMBERS, HALF, LON), F32)
            grad[slot, :, pl.ds(0, HALF), :] = jnp.zeros((MEMBERS, HALF, LON), F32)
            return carry

        lax.fori_loop(0, slots, clear, 0)

    @pl.when(jnp.logical_not(has_high))
    def _():
        def clear(slot, carry):
            raw[slot, :, pl.ds(HALF + ROWS, HALF), :] = jnp.zeros((MEMBERS, HALF, LON), F32)
            grad[slot, :, pl.ds(HALF + ROWS, HALF), :] = jnp.zeros((MEMBERS, HALF, LON), F32)
            return carry

        lax.fori_loop(0, slots, clear, 0)

    def push(source, target, send, recv, device):
        pltpu.make_async_remote_copy(
            src_ref=source,
            dst_ref=target,
            send_sem=send,
            recv_sem=recv,
            device_id=device,
            device_id_type=MESH,
        ).start()

    def send_halos(field, slot, low_send, low_recv, high_send, high_recv, stop, stop_recv):
        def piece(first, count, row):
            return field.at[slot, pl.ds(first, count), pl.ds(row, ROWS), :]

        def out_to(device, regions, row, send, recv, crossing):
            @pl.when(jnp.logical_not(crossing))
            def _():
                push(piece(0, MEMBERS, HALF), piece(0, MEMBERS, row), send, recv, device)

            @pl.when(crossing)
            def _():
                for n, region in enumerate(regions):
                    source = piece(STRAIGHT + n * PIECE, PIECE, HALF)
                    push(source, stop.at[slot], send, stop_recv.at[slot], (region, m))
                push(piece(0, STRAIGHT, HALF), piece(0, STRAIGHT, row), send, recv, device)

        @pl.when(has_high)
        def _():
            out_to(above(slot), UP_RELAYS, 0, high_send, high_recv.at[slot], at_top)

        @pl.when(has_low)
        def _():
            out_to(
                below(slot), DOWN_RELAYS, HALF + ROWS, low_send, low_recv.at[slot], at_bottom
            )

    def pass_on(field, slot, low_recv, high_recv, stop, stop_send, stop_recv):
        def forward(n, row, recv, device):
            part = stop.at[slot]
            pltpu.make_async_copy(part, part, stop_recv.at[slot]).wait()
            target = field.at[slot, pl.ds(STRAIGHT + n * PIECE, PIECE), pl.ds(row, HALF), :]
            push(part, target, stop_send, recv.at[slot], device)

        odd = lax.rem(slot, 2) == 1

        @pl.when(relay_up)
        def _():
            owner = jnp.where(odd, behind, m)
            forward((r == UP_RELAYS[1]).astype(jnp.int32), 0, high_recv, (TOP + 1, owner))

        @pl.when(relay_down)
        def _():
            owner = jnp.where(odd, ahead, m)
            forward((r == DOWN_RELAYS[1]).astype(jnp.int32), HALF + ROWS, low_recv, (TOP, owner))

    def wait_halos(field, slot, low_recv, high_recv):
        @pl.when(has_low)
        def _():
            part = field.at[slot, :, pl.ds(0, HALF), :]
            pltpu.make_async_copy(part, part, high_recv.at[slot]).wait()

        @pl.when(has_high)
        def _():
            part = field.at[slot, :, pl.ds(HALF + ROWS, HALF), :]
            pltpu.make_async_copy(part, part, low_recv.at[slot]).wait()

    def arrive(slot):
        part = raw.at[slot, :, pl.ds(HALF, ROWS), :]
        pltpu.make_async_copy(part, part, fwd_recv.at[slot]).wait()
        send_halos(raw, slot, down_send, down_recv, up_send, up_recv, way, way_recv)

    def middle(slot):
        wait_halos(raw, slot, down_recv, up_recv)
        smooth_lat(raw.at[slot], lat, mid)
        for block in range(4):
            rows = [mid[pl.ds(block * 8 + row, MEMBERS, stride=ROWS), :] for row in range(8)]
            cells[pl.ds(block * 256, 256), :] = smooth_lon(jnp.concatenate(rows, axis=0), lon)

        def pick_patch(k, carry):
            at = pl.multiple_of(k * MEMBERS, MEMBERS)
            picked[pl.ds(at, MEMBERS), :] = pick(cells, MEMBERS, rows_fwd, lanes_fwd, k)
            return carry

        lax.fori_loop(0, ROWS, pick_patch, 0, unroll=4)

        def quad(q, carry):
            at = pl.multiple_of(q * 4 * MEMBERS, 4 * MEMBERS)
            truths = jnp.stack(
                [fact_rows[pl.ds((4 * q + i) * 8 + slot, 1), :] for i in range(4)], axis=0
            )
            cells[pl.ds(at, 4 * MEMBERS), :] = pair_block(picked[pl.ds(at, 4 * MEMBERS), :], truths)
            return carry

        lax.fori_loop(0, ROWS // 4, quad, 0, unroll=2)

        def put_row(row, carry):
            at = pl.multiple_of(row * MEMBERS, MEMBERS)
            mid[pl.ds(at, MEMBERS), :] = pick(cells, MEMBERS, rows_inv, lanes_inv, row)
            return carry

        lax.fori_loop(0, ROWS, put_row, 0, unroll=4)
        for member in range(MEMBERS):
            grad[slot, member, pl.ds(HALF, ROWS), :] = mid[pl.ds(member, ROWS, stride=MEMBERS), :]

    def finish(slot):
        wait_halos(grad, slot, down2_recv, up2_recv)
        smooth_lat(grad.at[slot], lat, mid)
        for block in range(4):
            part = smooth_lon(mid[pl.ds(block * 256, 256), :], lon)
            done[slot, pl.ds(block * 8, 8)] = part.reshape(8, ROWS, LON)

    def give_back(slot):
        def to_peer(step, carry):
            peer = lax.rem(m + step, OWNERS)
            pltpu.make_async_remote_copy(
                src_ref=done.at[slot, pl.ds(2 * peer, 2)],
                dst_ref=out.at[:, variable(slot, m)],
                send_sem=ret_send,
                recv_sem=ret_recv,
                device_id=(r, peer),
                device_id_type=MESH,
            ).start()
            return carry

        lax.fori_loop(1, OWNERS, to_peer, 0, unroll=5)
        pltpu.make_async_copy(
            done.at[slot, pl.ds(2 * m, 2)], out.at[:, variable(slot, m)], ret_recv
        ).start()

    def step(i, carry):
        @pl.when(i + 1 < SLOTS - 1)
        def _():
            send_slot(i + 1, 0)

        @pl.when(i + 1 == SLOTS - 1)
        def _():
            send_slots_tail()

        @pl.when(jnp.logical_and(i >= 5, i < slots + 5))
        def _():
            give_back(i - 5)

        @pl.when(i < slots)
        def _():
            arrive(i)

        @pl.when(jnp.logical_and(i >= 2, i < slots + 2))
        def _():
            middle(i - 2)

        @pl.when(i < slots)
        def _():
            pass_on(raw, i, down_recv, up_recv, way, way_send, way_recv)

        @pl.when(jnp.logical_and(i >= 3, i < slots + 3))
        def _():
            pass_on(grad, i - 3, down2_recv, up2_recv, way2, way2_send, way2_recv)

        @pl.when(jnp.logical_and(i >= 4, i < slots + 4))
        def _():
            finish(i - 4)

        @pl.when(jnp.logical_and(i >= 2, i < slots + 2))
        def _():
            send_halos(grad, i - 2, down2_send, down2_recv, up2_send, up2_recv, way2, way2_recv)

        return carry

    lax.fori_loop(0, SLOTS + 5, step, 0)

    def drain(count):
        pltpu.make_async_copy(
            x.at[:, pl.ds(0, V - count)], x.at[:, pl.ds(0, V - count)], fwd_send
        ).wait()
        sent = done.at[pl.ds(0, count), pl.ds(0, 2 * OWNERS - 2)]
        pltpu.make_async_copy(sent, sent, ret_send).wait()

        @pl.when(jnp.logical_or(relay_up, relay_down))
        def _():
            for field, sem in ((way, way_send), (way2, way2_send)):
                part = field.at[pl.ds(0, count)]
                pltpu.make_async_copy(part, part, sem).wait()

        @pl.when(has_high)
        def _():
            for field, sem in ((raw, up_send), (grad, up2_send)):
                part = field.at[pl.ds(0, count), :, pl.ds(HALF, ROWS), :]
                pltpu.make_async_copy(part, part, sem).wait()

        @pl.when(has_low)
        def _():
            for field, sem in ((raw, down_send), (grad, down2_send)):
                part = field.at[pl.ds(0, count), :, pl.ds(HALF, ROWS), :]
                pltpu.make_async_copy(part, part, sem).wait()

    @pl.when(slots == SLOTS)
    def _():
        drain(SLOTS)

    @pl.when(slots != SLOTS)
    def _():
        drain(SLOTS - 1)

    pltpu.make_async_copy(out, out, ret_recv).wait()


def on_device(predicted_states, observed_analysis, tile_location_sequence):
    order = tile_location_sequence.reshape(ROWS, PATCH)
    dma = pltpu.SemaphoreType.DMA
    vmem = pl.BlockSpec(memory_space=pltpu.VMEM)
    hbm = pl.BlockSpec(memory_space=pl.ANY)
    return pl.pallas_call(
        kernel,
        out_shape=jax.ShapeDtypeStruct((2, V, ROWS, LON), F32),
        in_specs=[hbm, hbm, vmem, vmem, vmem],
        out_specs=hbm,
        scratch_shapes=[
            pltpu.VMEM((SLOTS, MEMBERS, SPAN, LON), F32),
            pltpu.VMEM((SLOTS, MEMBERS, SPAN, LON), F32),
            pltpu.VMEM((SLOTS, MEMBERS, ROWS, LON), F32),
            pltpu.VMEM((MEMBERS * ROWS, LON), F32),
            pltpu.VMEM((MEMBERS * ROWS, LON), F32),
            pltpu.VMEM((MEMBERS * ROWS, LON), F32),
            pltpu.VMEM((8, ROWS, LON), F32),
            pltpu.VMEM((8 * ROWS, LON), F32),
            pltpu.VMEM((ROWS, LON), jnp.int32),
            pltpu.VMEM((ROWS, LON), jnp.int32),
            pltpu.VMEM((ROWS, LON), jnp.int32),
            pltpu.VMEM((ROWS, LON), jnp.int32),
            dma(()), dma((SLOTS,)), dma(()), dma((SLOTS,)), dma(()), dma((SLOTS,)),
            dma(()), dma((SLOTS,)), dma(()), dma((SLOTS,)), dma(()), dma(()), dma(()),
            pltpu.VMEM((SLOTS, PIECE, HALF, LON), F32),
            pltpu.VMEM((SLOTS, PIECE, HALF, LON), F32),
            dma(()), dma((SLOTS,)), dma(()), dma((SLOTS,)),
        ],
        compiler_params=pltpu.CompilerParams(
            collective_id=0, has_side_effects=True, vmem_limit_bytes=56 * 1024 * 1024
        ),
    )(
        predicted_states,
        observed_analysis,
        order,
        jnp.asarray(lat_weights()),
        jnp.asarray(lon_weights()),
    )


def solution(mesh):
    in_specs = (P("member", None, "region", None), P(None, "region", None), P("region", None))
    out_specs = P("member", None, "region", None)
    return jax.shard_map(
        on_device, mesh=mesh, in_specs=in_specs, out_specs=out_specs, check_vma=False
    )
```

```python
import math

import jax
import jax.numpy as jnp
import numpy as np
from jax import lax
from jax.experimental import pallas as pl
from jax.experimental.pallas import tpu as pltpu
from jax.sharding import PartitionSpec as P

V = 100
ROWS = 32
LON = 128
HALF = 32
PATCH = 128
MEMBERS = 32
OWNERS = 16
REGIONS = 16
SLOTS = 7
SPAN = ROWS + 2 * HALF
CELLS = ROWS * LON
TOP = REGIONS // 2 - 1
UP_RELAYS = (4, 2)
DOWN_RELAYS = (11, 13)
RELAYS = 2
AWAY = 0
PIECE = 10
STRAIGHT = MEMBERS - RELAYS * PIECE
MESH = pl.DeviceIdType.MESH
F32 = jnp.float32
BF16 = jnp.bfloat16


def kernel_values(offset):
    sigma = HALF / 2.0
    steps = np.arange(-HALF, HALF + 1).astype(np.float64)
    norm = np.sum(np.exp(-(steps * steps) / (2.0 * sigma * sigma)))
    bell = np.exp(-(offset * offset) / (2.0 * sigma * sigma)) / norm
    value = 0.5 * (offset == 0.0) + 0.5 * bell
    return np.where(np.abs(offset) <= HALF, value, 0.0).astype(np.float32)


def halves(values):
    high = values.astype(BF16)
    low = (values - high.astype(np.float32)).astype(BF16)
    return high, low


def lat_weights():
    rows = np.arange(ROWS)[:, None]
    span = np.arange(SPAN)[None, :]
    high, low = halves(kernel_values((span - HALF - rows).astype(np.float64)))
    return np.concatenate(
        [np.concatenate([high, high], 1), np.concatenate([low, np.zeros_like(low)], 1)], 0
    )


def lon_weights():
    first = np.arange(LON)[:, None]
    second = np.arange(LON)[None, :]
    high, low = halves(kernel_values((second - first).astype(np.float64)))
    return np.concatenate(
        [np.concatenate([high, low], 1), np.concatenate([high, np.zeros_like(low)], 1)], 0
    )


def split(values):
    high = values.astype(BF16)
    low = (values - high.astype(F32)).astype(BF16)
    return high, low


def dot(a, b):
    return lax.dot_general(a, b, (((1,), (0,)), ((), ())), preferred_element_type=F32)


def dot_nt(a, b):
    return lax.dot_general(a, b, (((1,), (1,)), ((), ())), preferred_element_type=F32)


LANES = lax.GatherDimensionNumbers(
    offset_dims=(),
    collapsed_slice_dims=(1,),
    start_index_map=(1,),
    operand_batching_dims=(0,),
    start_indices_batching_dims=(0,),
)


def take_lanes(values, lanes):
    return lax.gather(
        values,
        lanes[..., None],
        LANES,
        slice_sizes=(1, 1),
        mode=lax.GatherScatterMode.PROMISE_IN_BOUNDS,
    )


def pick(src, group, row_of, lane_of, index):
    lanes = jnp.broadcast_to(lane_of[pl.ds(index, 1), :], (group, LON))
    rows = jnp.broadcast_to(row_of[pl.ds(index, 1), :], (group, LON))
    total = jnp.zeros((group, LON), F32)
    for row in range(ROWS):
        found = take_lanes(src[pl.ds(row * group, group), :], lanes)
        total = jnp.where(rows == row, found, total)
    return total


def smooth_lat(field, lat, mid):
    def pair(index, carry):
        both = jnp.concatenate([field[2 * index], field[2 * index + 1]], axis=1)
        high, low = split(both)
        parts = dot(lat[...], jnp.concatenate([high, low], axis=0))
        rows = parts[:ROWS] + parts[ROWS:]
        mid[pl.ds(pl.multiple_of(2 * index * ROWS, 64), ROWS), :] = rows[:, :LON]
        mid[pl.ds(pl.multiple_of(2 * index * ROWS + ROWS, 32), ROWS), :] = rows[:, LON:]
        return carry

    lax.fori_loop(0, MEMBERS // 2, pair, 0, unroll=2)


def smooth_lon(block, lon):
    high, low = split(block)
    parts = dot(jnp.concatenate([high, low], axis=1), lon[...])
    return parts[:, :LON] + parts[:, LON:]


def pair_block(a, truths):
    count = 4
    cube = a.reshape(count, MEMBERS, PATCH)
    mean = jnp.sum(cube, axis=1, keepdims=True) * (1.0 / MEMBERS)
    e = (cube - mean).reshape(count * MEMBERS, PATCH)
    d = (cube - truths).reshape(count * MEMBERS, PATCH)
    toward = d * lax.rsqrt(jnp.sum(d * d, axis=1, keepdims=True) + 1e-06)
    size = count * MEMBERS
    left = lax.broadcasted_iota(jnp.int32, (size, size), 0)
    right = lax.broadcasted_iota(jnp.int32, (size, size), 1)
    same = left == right
    other = jnp.logical_and(lax.div(left, MEMBERS) == lax.div(right, MEMBERS), left != right)
    high, low = split(e)
    gram = dot_nt(jnp.concatenate([high, low], axis=1), jnp.concatenate([high, high], axis=1))
    gram = gram + dot_nt(high, low)
    diagonal = jnp.where(same, gram, 0.0)
    dist = jnp.sum(diagonal, axis=1, keepdims=True) + jnp.sum(diagonal, axis=0, keepdims=True)
    dist = jnp.maximum(dist - 2.0 * gram, 0.0)
    weights = jnp.where(other, lax.rsqrt(dist + 1e-06), 0.0)
    pulled = jnp.sum(weights, axis=1, keepdims=True)
    mixing = jnp.where(same, pulled, -weights)
    mix_high, mix_low = split(mixing)
    apart = dot(jnp.concatenate([mix_high, mix_low], axis=1), jnp.concatenate([high, high], axis=0))
    apart = apart + dot(mix_high, low)
    return math.sqrt(PATCH) * (toward - apart * (1.0 / MEMBERS))


def kernel(
    x, truth, order, lat, lon, out,
    raw, grad, done, mid, cells, picked, facts, fact_rows, rows_fwd, lanes_fwd, rows_inv, lanes_inv,
    fwd_send, fwd_recv, up_send, up_recv, down_send, down_recv,
    up2_send, up2_recv, down2_send, down2_recv, ret_send, ret_recv, fact_sem,
    way, way2, way_send, way_recv, way2_send, way2_recv,
):
    r = lax.axis_index("region")
    m = lax.axis_index("member")
    slots = jnp.where(lax.rem(m, 5) == 0, SLOTS, SLOTS - 1)
    has_low = r > 0
    has_high = r < REGIONS - 1

    def turned(owner, by):
        return lax.div(owner, 4) * 4 + lax.rem(owner + 4 + by, 4)

    def variable(slot, owner):
        back = jnp.logical_and(lax.rem(slot, 2) == 1, r >= REGIONS // 2)
        place = jnp.where(back, turned(owner, 1), owner)
        return jnp.where(slot == SLOTS - 1, 96 + lax.div(owner, 5), slot * OWNERS + place)

    def above(slot):
        cross = jnp.logical_and(lax.rem(slot, 2) == 1, r == REGIONS // 2 - 1)
        return (r + 1, jnp.where(cross, turned(m, -1), m))

    def below(slot):
        cross = jnp.logical_and(lax.rem(slot, 2) == 1, r == REGIONS // 2)
        return (r - 1, jnp.where(cross, turned(m, 1), m))

    barrier = pltpu.get_barrier_semaphore()
    for step in range(1, OWNERS):
        peer = (r, lax.rem(m + step, OWNERS))
        pl.semaphore_signal(barrier, inc=1, device_id=peer, device_id_type=MESH)

    @pl.when(has_low)
    def _():
        pl.semaphore_signal(barrier, inc=1, device_id=(r - 1, m), device_id_type=MESH)

    @pl.when(has_high)
    def _():
        pl.semaphore_signal(barrier, inc=1, device_id=(r + 1, m), device_id_type=MESH)

    relay_up = jnp.logical_or(r == UP_RELAYS[0], r == UP_RELAYS[1])
    relay_down = jnp.logical_or(r == DOWN_RELAYS[0], r == DOWN_RELAYS[1])
    at_top = r == TOP
    at_bottom = r == TOP + 1
    ahead = turned(m, 1)
    behind = turned(m, -1)

    def greet(condition, peers):
        @pl.when(condition)
        def _():
            for peer in peers:
                pl.semaphore_signal(barrier, inc=1, device_id=peer, device_id_type=MESH)

        return condition.astype(jnp.int32) * len(peers)

    greeted = has_low.astype(jnp.int32) + has_high.astype(jnp.int32)
    greeted += greet(
        at_top,
        [(TOP + 1, behind)]
        + [(region, m) for region in UP_RELAYS]
        + [(region, who) for region in DOWN_RELAYS for who in (m, behind)],
    )
    greeted += greet(
        at_bottom,
        [(TOP, ahead)]
        + [(region, m) for region in DOWN_RELAYS]
        + [(region, who) for region in UP_RELAYS for who in (m, ahead)],
    )
    greeted += greet(relay_up, [(TOP, m), (TOP + 1, m), (TOP + 1, behind)])
    greeted += greet(relay_down, [(TOP + 1, m), (TOP, m), (TOP, ahead)])
    pl.semaphore_wait(barrier, OWNERS - 1 + greeted)

    def own_rows(slot):
        return raw.at[slot, pl.ds(2 * m, 2), pl.ds(HALF, ROWS), :]

    def send_block(slot, peer):
        pltpu.make_async_remote_copy(
            src_ref=x.at[:, variable(slot, peer)],
            dst_ref=own_rows(slot),
            send_sem=fwd_send,
            recv_sem=fwd_recv.at[slot],
            device_id=(r, peer),
            device_id_type=MESH,
        ).start()

    def send_slot(slot, carry):
        def to_peer(step, inner):
            send_block(slot, lax.rem(m + step, OWNERS))
            return inner

        return lax.fori_loop(1, OWNERS, to_peer, carry, unroll=5)

    lax.fori_loop(0, 1, send_slot, 0)

    def send_slots_tail():
        for index in range(4):

            @pl.when(m != 5 * index)
            def _(index=index):
                send_block(SLOTS - 1, 5 * index)

    def keep_slot(slot, carry):
        pltpu.make_async_copy(x.at[:, variable(slot, m)], own_rows(slot), fwd_recv.at[slot]).start()
        pltpu.make_async_copy(truth.at[variable(slot, m)], facts.at[slot], fact_sem).start()
        return carry

    lax.fori_loop(0, slots, keep_slot, 0)

    def invert(k, carry):
        cell = order[pl.ds(k, 1), :]
        row = lax.shift_right_logical(cell, 7)
        lane = jnp.bitwise_and(cell, LON - 1)
        rows_fwd[pl.ds(k, 1), :] = row
        lanes_fwd[pl.ds(k, 1), :] = lane
        at_row = lax.broadcasted_iota(jnp.int32, (ROWS, PATCH), 0) == row
        position = lax.broadcasted_iota(jnp.int32, (ROWS, PATCH), 1).astype(F32)
        patch = jnp.where(at_row, k.astype(F32), 0.0)
        place = jnp.where(at_row, position, 0.0)
        at_lane = lax.broadcasted_iota(jnp.int32, (LON, PATCH), 0) == lane
        chosen = jnp.where(at_lane, 1.0, 0.0).astype(BF16)
        return carry + dot_nt(jnp.concatenate([patch, place], axis=0).astype(BF16), chosen)

    inverse = lax.fori_loop(0, ROWS, invert, jnp.zeros((2 * ROWS, LON), F32), unroll=4)
    inverse = inverse.astype(jnp.int32)
    rows_inv[...] = inverse[:ROWS]
    lanes_inv[...] = inverse[ROWS:]

    @pl.when(slots == SLOTS)
    def _():
        pltpu.make_async_copy(facts.at[pl.ds(0, 7)], facts.at[pl.ds(0, 7)], fact_sem).wait()

    @pl.when(slots != SLOTS)
    def _():
        pltpu.make_async_copy(facts.at[pl.ds(0, 6)], facts.at[pl.ds(0, 6)], fact_sem).wait()

    for row in range(ROWS):
        fact_rows[pl.ds(row * 8, 8), :] = facts[:, row, :]

    def pick_fact(k, carry):
        picked[pl.ds(pl.multiple_of(k * 8, 8), 8), :] = pick(fact_rows, 8, rows_fwd, lanes_fwd, k)
        return carry

    lax.fori_loop(0, ROWS, pick_fact, 0, unroll=4)
    fact_rows[...] = picked[pl.ds(0, 8 * ROWS), :]

    @pl.when(jnp.logical_not(has_low))
    def _():
        def clear(slot, carry):
            raw[slot, :, pl.ds(0, HALF), :] = jnp.zeros((MEMBERS, HALF, LON), F32)
            grad[slot, :, pl.ds(0, HALF), :] = jnp.zeros((MEMBERS, HALF, LON), F32)
            return carry

        lax.fori_loop(0, slots, clear, 0)

    @pl.when(jnp.logical_not(has_high))
    def _():
        def clear(slot, carry):
            raw[slot, :, pl.ds(HALF + ROWS, HALF), :] = jnp.zeros((MEMBERS, HALF, LON), F32)
            grad[slot, :, pl.ds(HALF + ROWS, HALF), :] = jnp.zeros((MEMBERS, HALF, LON), F32)
            return carry

        lax.fori_loop(0, slots, clear, 0)

    def push(source, target, send, recv, device):
        pltpu.make_async_remote_copy(
            src_ref=source,
            dst_ref=target,
            send_sem=send,
            recv_sem=recv,
            device_id=device,
            device_id_type=MESH,
        ).start()

    def send_halos(field, slot, low_send, low_recv, high_send, high_recv, stop, stop_recv):
        def piece(first, count, row):
            return field.at[slot, pl.ds(first, count), pl.ds(row, ROWS), :]

        def out_to(device, regions, row, send, recv, crossing):
            @pl.when(jnp.logical_not(crossing))
            def _():
                push(piece(0, MEMBERS, HALF), piece(0, MEMBERS, row), send, recv, device)

            @pl.when(crossing)
            def _():
                for n, region in enumerate(regions):
                    source = piece(STRAIGHT + n * PIECE, PIECE, HALF)
                    push(source, stop.at[slot], send, stop_recv.at[slot], (region, m))
                push(piece(0, STRAIGHT, HALF), piece(0, STRAIGHT, row), send, recv, device)

        @pl.when(has_high)
        def _():
            out_to(above(slot), UP_RELAYS, 0, high_send, high_recv.at[slot], at_top)

        @pl.when(has_low)
        def _():
            out_to(
                below(slot), DOWN_RELAYS, HALF + ROWS, low_send, low_recv.at[slot], at_bottom
            )

    def pass_on(field, slot, low_recv, high_recv, stop, stop_send, stop_recv):
        def forward(n, row, recv, device):
            part = stop.at[slot]
            pltpu.make_async_copy(part, part, stop_recv.at[slot]).wait()
            target = field.at[slot, pl.ds(STRAIGHT + n * PIECE, PIECE), pl.ds(row, HALF), :]
            push(part, target, stop_send, recv.at[slot], device)

        odd = lax.rem(slot, 2) == 1

        @pl.when(relay_up)
        def _():
            owner = jnp.where(odd, behind, m)
            forward((r == UP_RELAYS[1]).astype(jnp.int32), 0, high_recv, (TOP + 1, owner))

        @pl.when(relay_down)
        def _():
            owner = jnp.where(odd, ahead, m)
            forward((r == DOWN_RELAYS[1]).astype(jnp.int32), HALF + ROWS, low_recv, (TOP, owner))

    def wait_halos(field, slot, low_recv, high_recv):
        @pl.when(has_low)
        def _():
            part = field.at[slot, :, pl.ds(0, HALF), :]
            pltpu.make_async_copy(part, part, high_recv.at[slot]).wait()

        @pl.when(has_high)
        def _():
            part = field.at[slot, :, pl.ds(HALF + ROWS, HALF), :]
            pltpu.make_async_copy(part, part, low_recv.at[slot]).wait()

    def arrive(slot):
        part = raw.at[slot, :, pl.ds(HALF, ROWS), :]
        pltpu.make_async_copy(part, part, fwd_recv.at[slot]).wait()
        send_halos(raw, slot, down_send, down_recv, up_send, up_recv, way, way_recv)

    def middle(slot):
        wait_halos(raw, slot, down_recv, up_recv)
        smooth_lat(raw.at[slot], lat, mid)
        for block in range(4):
            rows = [mid[pl.ds(block * 8 + row, MEMBERS, stride=ROWS), :] for row in range(8)]
            cells[pl.ds(block * 256, 256), :] = smooth_lon(jnp.concatenate(rows, axis=0), lon)

        def pick_patch(k, carry):
            at = pl.multiple_of(k * MEMBERS, MEMBERS)
            picked[pl.ds(at, MEMBERS), :] = pick(cells, MEMBERS, rows_fwd, lanes_fwd, k)
            return carry

        lax.fori_loop(0, ROWS, pick_patch, 0, unroll=4)

        def quad(q, carry):
            at = pl.multiple_of(q * 4 * MEMBERS, 4 * MEMBERS)
            truths = jnp.stack(
                [fact_rows[pl.ds((4 * q + i) * 8 + slot, 1), :] for i in range(4)], axis=0
            )
            cells[pl.ds(at, 4 * MEMBERS), :] = pair_block(picked[pl.ds(at, 4 * MEMBERS), :], truths)
            return carry

        lax.fori_loop(0, ROWS // 4, quad, 0, unroll=2)

        def put_row(row, carry):
            at = pl.multiple_of(row * MEMBERS, MEMBERS)
            mid[pl.ds(at, MEMBERS), :] = pick(cells, MEMBERS, rows_inv, lanes_inv, row)
            return carry

        lax.fori_loop(0, ROWS, put_row, 0, unroll=4)
        for member in range(MEMBERS):
            grad[slot, member, pl.ds(HALF, ROWS), :] = mid[pl.ds(member, ROWS, stride=MEMBERS), :]

    def finish(slot):
        wait_halos(grad, slot, down2_recv, up2_recv)
        smooth_lat(grad.at[slot], lat, mid)
        for block in range(4):
            part = smooth_lon(mid[pl.ds(block * 256, 256), :], lon)
            done[slot, pl.ds(block * 8, 8)] = part.reshape(8, ROWS, LON)

    def give_back(slot):
        def to_peer(step, carry):
            peer = lax.rem(m + step, OWNERS)
            pltpu.make_async_remote_copy(
                src_ref=done.at[slot, pl.ds(2 * peer, 2)],
                dst_ref=out.at[:, variable(slot, m)],
                send_sem=ret_send,
                recv_sem=ret_recv,
                device_id=(r, peer),
                device_id_type=MESH,
            ).start()
            return carry

        lax.fori_loop(1, OWNERS, to_peer, 0, unroll=5)
        pltpu.make_async_copy(
            done.at[slot, pl.ds(2 * m, 2)], out.at[:, variable(slot, m)], ret_recv
        ).start()

    def step(i, carry):
        @pl.when(i + 1 < SLOTS - 1)
        def _():
            send_slot(i + 1, 0)

        @pl.when(i + 1 == SLOTS - 1)
        def _():
            send_slots_tail()

        @pl.when(jnp.logical_and(i >= 5, i < slots + 5))
        def _():
            give_back(i - 5)

        @pl.when(jnp.logical_and(i < slots, i != 2))
        def _():
            arrive(i)

        @pl.when(jnp.logical_and(i >= 2, i < slots + 2))
        def _():
            middle(i - 2)

        @pl.when(i == 2)
        def _():
            arrive(i)

        @pl.when(i < slots)
        def _():
            pass_on(raw, i, down_recv, up_recv, way, way_send, way_recv)

        @pl.when(jnp.logical_and(i >= 3, i < slots + 3))
        def _():
            pass_on(grad, i - 3, down2_recv, up2_recv, way2, way2_send, way2_recv)

        @pl.when(jnp.logical_and(i >= 4, i < slots + 4))
        def _():
            finish(i - 4)

        @pl.when(jnp.logical_and(i >= 2, i < slots + 2))
        def _():
            send_halos(grad, i - 2, down2_send, down2_recv, up2_send, up2_recv, way2, way2_recv)

        return carry

    lax.fori_loop(0, SLOTS + 5, step, 0)

    def drain(count):
        pltpu.make_async_copy(
            x.at[:, pl.ds(0, V - count)], x.at[:, pl.ds(0, V - count)], fwd_send
        ).wait()
        sent = done.at[pl.ds(0, count), pl.ds(0, 2 * OWNERS - 2)]
        pltpu.make_async_copy(sent, sent, ret_send).wait()

        @pl.when(jnp.logical_or(relay_up, relay_down))
        def _():
            for field, sem in ((way, way_send), (way2, way2_send)):
                part = field.at[pl.ds(0, count)]
                pltpu.make_async_copy(part, part, sem).wait()

        @pl.when(has_high)
        def _():
            for field, sem in ((raw, up_send), (grad, up2_send)):
                part = field.at[pl.ds(0, count), :, pl.ds(HALF, ROWS), :]
                pltpu.make_async_copy(part, part, sem).wait()

        @pl.when(has_low)
        def _():
            for field, sem in ((raw, down_send), (grad, down2_send)):
                part = field.at[pl.ds(0, count), :, pl.ds(HALF, ROWS), :]
                pltpu.make_async_copy(part, part, sem).wait()

    @pl.when(slots == SLOTS)
    def _():
        drain(SLOTS)

    @pl.when(slots != SLOTS)
    def _():
        drain(SLOTS - 1)

    pltpu.make_async_copy(out, out, ret_recv).wait()


def on_device(predicted_states, observed_analysis, tile_location_sequence):
    order = tile_location_sequence.reshape(ROWS, PATCH)
    dma = pltpu.SemaphoreType.DMA
    vmem = pl.BlockSpec(memory_space=pltpu.VMEM)
    hbm = pl.BlockSpec(memory_space=pl.ANY)
    return pl.pallas_call(
        kernel,
        out_shape=jax.ShapeDtypeStruct((2, V, ROWS, LON), F32),
        in_specs=[hbm, hbm, vmem, vmem, vmem],
        out_specs=hbm,
        scratch_shapes=[
            pltpu.VMEM((SLOTS, MEMBERS, SPAN, LON), F32),
            pltpu.VMEM((SLOTS, MEMBERS, SPAN, LON), F32),
            pltpu.VMEM((SLOTS, MEMBERS, ROWS, LON), F32),
            pltpu.VMEM((MEMBERS * ROWS, LON), F32),
            pltpu.VMEM((MEMBERS * ROWS, LON), F32),
            pltpu.VMEM((MEMBERS * ROWS, LON), F32),
            pltpu.VMEM((8, ROWS, LON), F32),
            pltpu.VMEM((8 * ROWS, LON), F32),
            pltpu.VMEM((ROWS, LON), jnp.int32),
            pltpu.VMEM((ROWS, LON), jnp.int32),
            pltpu.VMEM((ROWS, LON), jnp.int32),
            pltpu.VMEM((ROWS, LON), jnp.int32),
            dma(()), dma((SLOTS,)), dma(()), dma((SLOTS,)), dma(()), dma((SLOTS,)),
            dma(()), dma((SLOTS,)), dma(()), dma((SLOTS,)), dma(()), dma(()), dma(()),
            pltpu.VMEM((SLOTS, PIECE, HALF, LON), F32),
            pltpu.VMEM((SLOTS, PIECE, HALF, LON), F32),
            dma(()), dma((SLOTS,)), dma(()), dma((SLOTS,)),
        ],
        compiler_params=pltpu.CompilerParams(
            collective_id=0, has_side_effects=True, vmem_limit_bytes=56 * 1024 * 1024
        ),
    )(
        predicted_states,
        observed_analysis,
        order,
        jnp.asarray(lat_weights()),
        jnp.asarray(lon_weights()),
    )


def solution(mesh):
    in_specs = (P("member", None, "region", None), P(None, "region", None), P("region", None))
    out_specs = P("member", None, "region", None)
    return jax.shard_map(
        on_device, mesh=mesh, in_specs=in_specs, out_specs=out_specs, check_vma=False
    )
```

```python
import math

import jax
import jax.numpy as jnp
import numpy as np
from jax import lax
from jax.experimental import pallas as pl
from jax.experimental.pallas import tpu as pltpu
from jax.sharding import PartitionSpec as P

V = 100
ROWS = 32
LON = 128
HALF = 32
PATCH = 128
MEMBERS = 32
OWNERS = 16
REGIONS = 16
SLOTS = 7
SPAN = ROWS + 2 * HALF
CELLS = ROWS * LON
TOP = REGIONS // 2 - 1
UP_RELAYS = (4, 2)
DOWN_RELAYS = (11, 13)
RELAYS = 2
AWAY = 0
PIECE = 12
STRAIGHT = MEMBERS - RELAYS * PIECE
MESH = pl.DeviceIdType.MESH
F32 = jnp.float32
BF16 = jnp.bfloat16


def kernel_values(offset):
    sigma = HALF / 2.0
    steps = np.arange(-HALF, HALF + 1).astype(np.float64)
    norm = np.sum(np.exp(-(steps * steps) / (2.0 * sigma * sigma)))
    bell = np.exp(-(offset * offset) / (2.0 * sigma * sigma)) / norm
    value = 0.5 * (offset == 0.0) + 0.5 * bell
    return np.where(np.abs(offset) <= HALF, value, 0.0).astype(np.float32)


def halves(values):
    high = values.astype(BF16)
    low = (values - high.astype(np.float32)).astype(BF16)
    return high, low


def lat_weights():
    rows = np.arange(ROWS)[:, None]
    span = np.arange(SPAN)[None, :]
    high, low = halves(kernel_values((span - HALF - rows).astype(np.float64)))
    return np.concatenate(
        [np.concatenate([high, high], 1), np.concatenate([low, np.zeros_like(low)], 1)], 0
    )


def lon_weights():
    first = np.arange(LON)[:, None]
    second = np.arange(LON)[None, :]
    high, low = halves(kernel_values((second - first).astype(np.float64)))
    return np.concatenate(
        [np.concatenate([high, low], 1), np.concatenate([high, np.zeros_like(low)], 1)], 0
    )


def split(values):
    high = values.astype(BF16)
    low = (values - high.astype(F32)).astype(BF16)
    return high, low


def dot(a, b):
    return lax.dot_general(a, b, (((1,), (0,)), ((), ())), preferred_element_type=F32)


def dot_nt(a, b):
    return lax.dot_general(a, b, (((1,), (1,)), ((), ())), preferred_element_type=F32)


LANES = lax.GatherDimensionNumbers(
    offset_dims=(),
    collapsed_slice_dims=(1,),
    start_index_map=(1,),
    operand_batching_dims=(0,),
    start_indices_batching_dims=(0,),
)


def take_lanes(values, lanes):
    return lax.gather(
        values,
        lanes[..., None],
        LANES,
        slice_sizes=(1, 1),
        mode=lax.GatherScatterMode.PROMISE_IN_BOUNDS,
    )


def pick(src, group, row_of, lane_of, index):
    lanes = jnp.broadcast_to(lane_of[pl.ds(index, 1), :], (group, LON))
    rows = jnp.broadcast_to(row_of[pl.ds(index, 1), :], (group, LON))
    total = jnp.zeros((group, LON), F32)
    for row in range(ROWS):
        found = take_lanes(src[pl.ds(row * group, group), :], lanes)
        total = jnp.where(rows == row, found, total)
    return total


def smooth_lat(field, lat, mid):
    def pair(index, carry):
        both = jnp.concatenate([field[2 * index], field[2 * index + 1]], axis=1)
        high, low = split(both)
        parts = dot(lat[...], jnp.concatenate([high, low], axis=0))
        rows = parts[:ROWS] + parts[ROWS:]
        mid[pl.ds(pl.multiple_of(2 * index * ROWS, 64), ROWS), :] = rows[:, :LON]
        mid[pl.ds(pl.multiple_of(2 * index * ROWS + ROWS, 32), ROWS), :] = rows[:, LON:]
        return carry

    lax.fori_loop(0, MEMBERS // 2, pair, 0, unroll=2)


def smooth_lon(block, lon):
    high, low = split(block)
    parts = dot(jnp.concatenate([high, low], axis=1), lon[...])
    return parts[:, :LON] + parts[:, LON:]


def pair_block(a, truths):
    count = 4
    cube = a.reshape(count, MEMBERS, PATCH)
    mean = jnp.sum(cube, axis=1, keepdims=True) * (1.0 / MEMBERS)
    e = (cube - mean).reshape(count * MEMBERS, PATCH)
    d = (cube - truths).reshape(count * MEMBERS, PATCH)
    toward = d * lax.rsqrt(jnp.sum(d * d, axis=1, keepdims=True) + 1e-06)
    size = count * MEMBERS
    left = lax.broadcasted_iota(jnp.int32, (size, size), 0)
    right = lax.broadcasted_iota(jnp.int32, (size, size), 1)
    same = left == right
    other = jnp.logical_and(lax.div(left, MEMBERS) == lax.div(right, MEMBERS), left != right)
    high, low = split(e)
    gram = dot_nt(jnp.concatenate([high, low], axis=1), jnp.concatenate([high, high], axis=1))
    gram = gram + dot_nt(high, low)
    diagonal = jnp.where(same, gram, 0.0)
    dist = jnp.sum(diagonal, axis=1, keepdims=True) + jnp.sum(diagonal, axis=0, keepdims=True)
    dist = jnp.maximum(dist - 2.0 * gram, 0.0)
    weights = jnp.where(other, lax.rsqrt(dist + 1e-06), 0.0)
    pulled = jnp.sum(weights, axis=1, keepdims=True)
    mixing = jnp.where(same, pulled, -weights)
    mix_high, mix_low = split(mixing)
    apart = dot(jnp.concatenate([mix_high, mix_low], axis=1), jnp.concatenate([high, high], axis=0))
    apart = apart + dot(mix_high, low)
    return math.sqrt(PATCH) * (toward - apart * (1.0 / MEMBERS))


def kernel(
    x, truth, order, lat, lon, out,
    raw, grad, done, mid, cells, picked, facts, fact_rows, rows_fwd, lanes_fwd, rows_inv, lanes_inv,
    fwd_send, fwd_recv, up_send, up_recv, down_send, down_recv,
    up2_send, up2_recv, down2_send, down2_recv, ret_send, ret_recv, fact_sem,
    way, way2, way_send, way_recv, way2_send, way2_recv,
):
    r = lax.axis_index("region")
    m = lax.axis_index("member")
    slots = jnp.where(lax.rem(m, 5) == 0, SLOTS, SLOTS - 1)
    has_low = r > 0
    has_high = r < REGIONS - 1

    def turned(owner, by):
        return lax.div(owner, 4) * 4 + lax.rem(owner + 4 + by, 4)

    def variable(slot, owner):
        back = jnp.logical_and(lax.rem(slot, 2) == 1, r >= REGIONS // 2)
        place = jnp.where(back, turned(owner, 1), owner)
        return jnp.where(slot == SLOTS - 1, 96 + lax.div(owner, 5), slot * OWNERS + place)

    def above(slot):
        cross = jnp.logical_and(lax.rem(slot, 2) == 1, r == REGIONS // 2 - 1)
        return (r + 1, jnp.where(cross, turned(m, -1), m))

    def below(slot):
        cross = jnp.logical_and(lax.rem(slot, 2) == 1, r == REGIONS // 2)
        return (r - 1, jnp.where(cross, turned(m, 1), m))

    barrier = pltpu.get_barrier_semaphore()
    for step in range(1, OWNERS):
        peer = (r, lax.rem(m + step, OWNERS))
        pl.semaphore_signal(barrier, inc=1, device_id=peer, device_id_type=MESH)

    @pl.when(has_low)
    def _():
        pl.semaphore_signal(barrier, inc=1, device_id=(r - 1, m), device_id_type=MESH)

    @pl.when(has_high)
    def _():
        pl.semaphore_signal(barrier, inc=1, device_id=(r + 1, m), device_id_type=MESH)

    relay_up = jnp.logical_or(r == UP_RELAYS[0], r == UP_RELAYS[1])
    relay_down = jnp.logical_or(r == DOWN_RELAYS[0], r == DOWN_RELAYS[1])
    at_top = r == TOP
    at_bottom = r == TOP + 1
    ahead = turned(m, 1)
    behind = turned(m, -1)

    def greet(condition, peers):
        @pl.when(condition)
        def _():
            for peer in peers:
                pl.semaphore_signal(barrier, inc=1, device_id=peer, device_id_type=MESH)

        return condition.astype(jnp.int32) * len(peers)

    greeted = has_low.astype(jnp.int32) + has_high.astype(jnp.int32)
    greeted += greet(
        at_top,
        [(TOP + 1, behind)]
        + [(region, m) for region in UP_RELAYS]
        + [(region, who) for region in DOWN_RELAYS for who in (m, behind)],
    )
    greeted += greet(
        at_bottom,
        [(TOP, ahead)]
        + [(region, m) for region in DOWN_RELAYS]
        + [(region, who) for region in UP_RELAYS for who in (m, ahead)],
    )
    greeted += greet(relay_up, [(TOP, m), (TOP + 1, m), (TOP + 1, behind)])
    greeted += greet(relay_down, [(TOP + 1, m), (TOP, m), (TOP, ahead)])
    pl.semaphore_wait(barrier, OWNERS - 1 + greeted)

    def own_rows(slot):
        return raw.at[slot, pl.ds(2 * m, 2), pl.ds(HALF, ROWS), :]

    def send_block(slot, peer):
        pltpu.make_async_remote_copy(
            src_ref=x.at[:, variable(slot, peer)],
            dst_ref=own_rows(slot),
            send_sem=fwd_send,
            recv_sem=fwd_recv.at[slot],
            device_id=(r, peer),
            device_id_type=MESH,
        ).start()

    def send_slot(slot, carry):
        def to_peer(step, inner):
            send_block(slot, lax.rem(m + step, OWNERS))
            return inner

        return lax.fori_loop(1, OWNERS, to_peer, carry, unroll=5)

    lax.fori_loop(0, 1, send_slot, 0)

    def send_slots_tail():
        for index in range(4):

            @pl.when(m != 5 * index)
            def _(index=index):
                send_block(SLOTS - 1, 5 * index)

    def keep_slot(slot, carry):
        pltpu.make_async_copy(x.at[:, variable(slot, m)], own_rows(slot), fwd_recv.at[slot]).start()
        pltpu.make_async_copy(truth.at[variable(slot, m)], facts.at[slot], fact_sem).start()
        return carry

    lax.fori_loop(0, slots, keep_slot, 0)

    def invert(k, carry):
        cell = order[pl.ds(k, 1), :]
        row = lax.shift_right_logical(cell, 7)
        lane = jnp.bitwise_and(cell, LON - 1)
        rows_fwd[pl.ds(k, 1), :] = row
        lanes_fwd[pl.ds(k, 1), :] = lane
        at_row = lax.broadcasted_iota(jnp.int32, (ROWS, PATCH), 0) == row
        position = lax.broadcasted_iota(jnp.int32, (ROWS, PATCH), 1).astype(F32)
        patch = jnp.where(at_row, k.astype(F32), 0.0)
        place = jnp.where(at_row, position, 0.0)
        at_lane = lax.broadcasted_iota(jnp.int32, (LON, PATCH), 0) == lane
        chosen = jnp.where(at_lane, 1.0, 0.0).astype(BF16)
        return carry + dot_nt(jnp.concatenate([patch, place], axis=0).astype(BF16), chosen)

    inverse = lax.fori_loop(0, ROWS, invert, jnp.zeros((2 * ROWS, LON), F32), unroll=4)
    inverse = inverse.astype(jnp.int32)
    rows_inv[...] = inverse[:ROWS]
    lanes_inv[...] = inverse[ROWS:]

    @pl.when(slots == SLOTS)
    def _():
        pltpu.make_async_copy(facts.at[pl.ds(0, 7)], facts.at[pl.ds(0, 7)], fact_sem).wait()

    @pl.when(slots != SLOTS)
    def _():
        pltpu.make_async_copy(facts.at[pl.ds(0, 6)], facts.at[pl.ds(0, 6)], fact_sem).wait()

    for row in range(ROWS):
        fact_rows[pl.ds(row * 8, 8), :] = facts[:, row, :]

    def pick_fact(k, carry):
        picked[pl.ds(pl.multiple_of(k * 8, 8), 8), :] = pick(fact_rows, 8, rows_fwd, lanes_fwd, k)
        return carry

    lax.fori_loop(0, ROWS, pick_fact, 0, unroll=4)
    fact_rows[...] = picked[pl.ds(0, 8 * ROWS), :]

    @pl.when(jnp.logical_not(has_low))
    def _():
        def clear(slot, carry):
            raw[slot, :, pl.ds(0, HALF), :] = jnp.zeros((MEMBERS, HALF, LON), F32)
            grad[slot, :, pl.ds(0, HALF), :] = jnp.zeros((MEMBERS, HALF, LON), F32)
            return carry

        lax.fori_loop(0, slots, clear, 0)

    @pl.when(jnp.logical_not(has_high))
    def _():
        def clear(slot, carry):
            raw[slot, :, pl.ds(HALF + ROWS, HALF), :] = jnp.zeros((MEMBERS, HALF, LON), F32)
            grad[slot, :, pl.ds(HALF + ROWS, HALF), :] = jnp.zeros((MEMBERS, HALF, LON), F32)
            return carry

        lax.fori_loop(0, slots, clear, 0)

    def push(source, target, send, recv, device):
        pltpu.make_async_remote_copy(
            src_ref=source,
            dst_ref=target,
            send_sem=send,
            recv_sem=recv,
            device_id=device,
            device_id_type=MESH,
        ).start()

    def send_halos(field, slot, low_send, low_recv, high_send, high_recv, stop, stop_recv):
        def piece(first, count, row):
            return field.at[slot, pl.ds(first, count), pl.ds(row, ROWS), :]

        def out_to(device, regions, row, send, recv, crossing):
            @pl.when(jnp.logical_not(crossing))
            def _():
                push(piece(0, MEMBERS, HALF), piece(0, MEMBERS, row), send, recv, device)

            @pl.when(crossing)
            def _():
                for n, region in enumerate(regions):
                    source = piece(STRAIGHT + n * PIECE, PIECE, HALF)
                    push(source, stop.at[slot], send, stop_recv.at[slot], (region, m))
                push(piece(0, STRAIGHT, HALF), piece(0, STRAIGHT, row), send, recv, device)

        @pl.when(has_high)
        def _():
            out_to(above(slot), UP_RELAYS, 0, high_send, high_recv.at[slot], at_top)

        @pl.when(has_low)
        def _():
            out_to(
                below(slot), DOWN_RELAYS, HALF + ROWS, low_send, low_recv.at[slot], at_bottom
            )

    def pass_on(field, slot, low_recv, high_recv, stop, stop_send, stop_recv):
        def forward(n, row, recv, device):
            part = stop.at[slot]
            pltpu.make_async_copy(part, part, stop_recv.at[slot]).wait()
            target = field.at[slot, pl.ds(STRAIGHT + n * PIECE, PIECE), pl.ds(row, HALF), :]
            push(part, target, stop_send, recv.at[slot], device)

        odd = lax.rem(slot, 2) == 1

        @pl.when(relay_up)
        def _():
            owner = jnp.where(odd, behind, m)
            forward((r == UP_RELAYS[1]).astype(jnp.int32), 0, high_recv, (TOP + 1, owner))

        @pl.when(relay_down)
        def _():
            owner = jnp.where(odd, ahead, m)
            forward((r == DOWN_RELAYS[1]).astype(jnp.int32), HALF + ROWS, low_recv, (TOP, owner))

    def wait_halos(field, slot, low_recv, high_recv):
        @pl.when(has_low)
        def _():
            part = field.at[slot, :, pl.ds(0, HALF), :]
            pltpu.make_async_copy(part, part, high_recv.at[slot]).wait()

        @pl.when(has_high)
        def _():
            part = field.at[slot, :, pl.ds(HALF + ROWS, HALF), :]
            pltpu.make_async_copy(part, part, low_recv.at[slot]).wait()

    def arrive(slot):
        part = raw.at[slot, :, pl.ds(HALF, ROWS), :]
        pltpu.make_async_copy(part, part, fwd_recv.at[slot]).wait()
        send_halos(raw, slot, down_send, down_recv, up_send, up_recv, way, way_recv)

    def middle(slot):
        wait_halos(raw, slot, down_recv, up_recv)
        smooth_lat(raw.at[slot], lat, mid)
        for block in range(4):
            rows = [mid[pl.ds(block * 8 + row, MEMBERS, stride=ROWS), :] for row in range(8)]
            cells[pl.ds(block * 256, 256), :] = smooth_lon(jnp.concatenate(rows, axis=0), lon)

        def pick_patch(k, carry):
            at = pl.multiple_of(k * MEMBERS, MEMBERS)
            picked[pl.ds(at, MEMBERS), :] = pick(cells, MEMBERS, rows_fwd, lanes_fwd, k)
            return carry

        lax.fori_loop(0, ROWS, pick_patch, 0, unroll=4)

        def quad(q, carry):
            at = pl.multiple_of(q * 4 * MEMBERS, 4 * MEMBERS)
            truths = jnp.stack(
                [fact_rows[pl.ds((4 * q + i) * 8 + slot, 1), :] for i in range(4)], axis=0
            )
            cells[pl.ds(at, 4 * MEMBERS), :] = pair_block(picked[pl.ds(at, 4 * MEMBERS), :], truths)
            return carry

        lax.fori_loop(0, ROWS // 4, quad, 0, unroll=2)

        def put_row(row, carry):
            at = pl.multiple_of(row * MEMBERS, MEMBERS)
            mid[pl.ds(at, MEMBERS), :] = pick(cells, MEMBERS, rows_inv, lanes_inv, row)
            return carry

        lax.fori_loop(0, ROWS, put_row, 0, unroll=4)
        for member in range(MEMBERS):
            grad[slot, member, pl.ds(HALF, ROWS), :] = mid[pl.ds(member, ROWS, stride=MEMBERS), :]

    def finish(slot):
        wait_halos(grad, slot, down2_recv, up2_recv)
        smooth_lat(grad.at[slot], lat, mid)
        for block in range(4):
            part = smooth_lon(mid[pl.ds(block * 256, 256), :], lon)
            done[slot, pl.ds(block * 8, 8)] = part.reshape(8, ROWS, LON)

    def give_back(slot):
        def to_peer(step, carry):
            peer = lax.rem(m + step, OWNERS)
            pltpu.make_async_remote_copy(
                src_ref=done.at[slot, pl.ds(2 * peer, 2)],
                dst_ref=out.at[:, variable(slot, m)],
                send_sem=ret_send,
                recv_sem=ret_recv,
                device_id=(r, peer),
                device_id_type=MESH,
            ).start()
            return carry

        lax.fori_loop(1, OWNERS, to_peer, 0, unroll=5)
        pltpu.make_async_copy(
            done.at[slot, pl.ds(2 * m, 2)], out.at[:, variable(slot, m)], ret_recv
        ).start()

    def step(i, carry):
        @pl.when(i + 1 < SLOTS - 1)
        def _():
            send_slot(i + 1, 0)

        @pl.when(i + 1 == SLOTS - 1)
        def _():
            send_slots_tail()

        @pl.when(jnp.logical_and(i >= 5, i < slots + 5))
        def _():
            give_back(i - 5)

        @pl.when(jnp.logical_and(i < slots, i != 2))
        def _():
            arrive(i)

        @pl.when(jnp.logical_and(i >= 2, i < slots + 2))
        def _():
            middle(i - 2)

        @pl.when(i == 2)
        def _():
            arrive(i)

        @pl.when(i < slots)
        def _():
            pass_on(raw, i, down_recv, up_recv, way, way_send, way_recv)

        @pl.when(jnp.logical_and(i >= 3, i < slots + 3))
        def _():
            pass_on(grad, i - 3, down2_recv, up2_recv, way2, way2_send, way2_recv)

        @pl.when(jnp.logical_and(i >= 4, i < slots + 4))
        def _():
            finish(i - 4)

        @pl.when(jnp.logical_and(i >= 2, i < slots + 2))
        def _():
            send_halos(grad, i - 2, down2_send, down2_recv, up2_send, up2_recv, way2, way2_recv)

        return carry

    lax.fori_loop(0, SLOTS + 5, step, 0)

    def drain(count):
        pltpu.make_async_copy(
            x.at[:, pl.ds(0, V - count)], x.at[:, pl.ds(0, V - count)], fwd_send
        ).wait()
        sent = done.at[pl.ds(0, count), pl.ds(0, 2 * OWNERS - 2)]
        pltpu.make_async_copy(sent, sent, ret_send).wait()

        @pl.when(jnp.logical_or(relay_up, relay_down))
        def _():
            for field, sem in ((way, way_send), (way2, way2_send)):
                part = field.at[pl.ds(0, count)]
                pltpu.make_async_copy(part, part, sem).wait()

        @pl.when(has_high)
        def _():
            for field, sem in ((raw, up_send), (grad, up2_send)):
                part = field.at[pl.ds(0, count), :, pl.ds(HALF, ROWS), :]
                pltpu.make_async_copy(part, part, sem).wait()

        @pl.when(has_low)
        def _():
            for field, sem in ((raw, down_send), (grad, down2_send)):
                part = field.at[pl.ds(0, count), :, pl.ds(HALF, ROWS), :]
                pltpu.make_async_copy(part, part, sem).wait()

    @pl.when(slots == SLOTS)
    def _():
        drain(SLOTS)

    @pl.when(slots != SLOTS)
    def _():
        drain(SLOTS - 1)

    pltpu.make_async_copy(out, out, ret_recv).wait()


def on_device(predicted_states, observed_analysis, tile_location_sequence):
    order = tile_location_sequence.reshape(ROWS, PATCH)
    dma = pltpu.SemaphoreType.DMA
    vmem = pl.BlockSpec(memory_space=pltpu.VMEM)
    hbm = pl.BlockSpec(memory_space=pl.ANY)
    return pl.pallas_call(
        kernel,
        out_shape=jax.ShapeDtypeStruct((2, V, ROWS, LON), F32),
        in_specs=[hbm, hbm, vmem, vmem, vmem],
        out_specs=hbm,
        scratch_shapes=[
            pltpu.VMEM((SLOTS, MEMBERS, SPAN, LON), F32),
            pltpu.VMEM((SLOTS, MEMBERS, SPAN, LON), F32),
            pltpu.VMEM((SLOTS, MEMBERS, ROWS, LON), F32),
            pltpu.VMEM((MEMBERS * ROWS, LON), F32),
            pltpu.VMEM((MEMBERS * ROWS, LON), F32),
            pltpu.VMEM((MEMBERS * ROWS, LON), F32),
            pltpu.VMEM((8, ROWS, LON), F32),
            pltpu.VMEM((8 * ROWS, LON), F32),
            pltpu.VMEM((ROWS, LON), jnp.int32),
            pltpu.VMEM((ROWS, LON), jnp.int32),
            pltpu.VMEM((ROWS, LON), jnp.int32),
            pltpu.VMEM((ROWS, LON), jnp.int32),
            dma(()), dma((SLOTS,)), dma(()), dma((SLOTS,)), dma(()), dma((SLOTS,)),
            dma(()), dma((SLOTS,)), dma(()), dma((SLOTS,)), dma(()), dma(()), dma(()),
            pltpu.VMEM((SLOTS, PIECE, HALF, LON), F32),
            pltpu.VMEM((SLOTS, PIECE, HALF, LON), F32),
            dma(()), dma((SLOTS,)), dma(()), dma((SLOTS,)),
        ],
        compiler_params=pltpu.CompilerParams(
            collective_id=0, has_side_effects=True, vmem_limit_bytes=56 * 1024 * 1024
        ),
    )(
        predicted_states,
        observed_analysis,
        order,
        jnp.asarray(lat_weights()),
        jnp.asarray(lon_weights()),
    )


def solution(mesh):
    in_specs = (P("member", None, "region", None), P(None, "region", None), P("region", None))
    out_specs = P("member", None, "region", None)
    return jax.shard_map(
        on_device, mesh=mesh, in_specs=in_specs, out_specs=out_specs, check_vma=False
    )
```
